512 devices in a mesh: plane: 64 (over x, z_lo, y), vert: 8 (over z_hi, core).
Axes of the slice: x: 4, y: 8, z: 8 (z_hi: 4, z_lo: 2; z = z_hi * 2 + z_lo), core: 2. Of those that a mesh axis runs over, the one named last changes fastest.
Arguments:
- source: float32 [128, 512, 512], P('vert', 'plane'), may hold values from -6 to 6
- inv_density: float32 [128, 512, 512], P('vert', 'plane'), may hold values from 0.1 to 10
- pressure: float32 [128, 512, 512], P('vert', 'plane'), may hold values from -6 to 6
Outputs:
- corrected: float32 [128, 512, 512], P('vert', 'plane')
The draws below stay inside these ranges and needn't reach their ends.
All inputs are finite; a program needn't handle non-finite values.
Results may differ from the reference program's by a relative error of at most 0.00002.
Values sent between devices are 32-bit elements; how exact they have to be, the bound alone decides.
A program may use at most 64 MiB of HBM per device.

```python
import math
import jax
import jax.numpy as jnp

NY = 512
LEVELS = 4
COARSE_SWEEPS = 4
NZ = 128
NX = 512


def shard_levels(stream_key, dims, pieces, smallest, top_value):
    gain, own = 1.0, jax.random.fold_in(stream_key, 6)
    for axis_at, blocks in pieces:
        draws = jnp.exp(jax.random.uniform(jax.random.fold_in(own, axis_at), (blocks,), jnp.float32, smallest / len(pieces), top_value / len(pieces)))
        gain = gain * jnp.repeat(draws, dims[axis_at] // blocks).reshape([-1 if axis == axis_at else 1 for axis in range(len(dims))])
    return gain


def scatter_about(key, extent, spread, most, split=(), kind=jnp.bfloat16):
    array = jax.random.normal(key, extent, jnp.float32) * spread
    if len(split) > 0:
        array = shard_levels(key, extent, split, -0.22, 0.18) * array
    return jnp.clip(array, min=-most, max=most).astype(kind)


def setup_inputs(seed: int = 0) -> dict:
    splits = jax.random.split(jax.random.key(seed), 4)
    return {
        "source": scatter_about(splits[0], (NZ, NX, NY), 1.0, 6.0, ((0, 8), (1, 64)), jnp.float32),
        "inv_density": jnp.clip(jnp.exp(math.log(10.0) - 4.6051702 * jax.random.uniform(splits[1], (NZ, NX, NY), jnp.float32) ** shard_levels(splits[1], (NZ, NX, NY), ((0, 8), (1, 64)), -0.2, 0.2)), 0.1, 10.0),
        "pressure": scatter_about(splits[2], (NZ, NX, NY), 1.0, 6.0, ((0, 8), (1, 64)), jnp.float32),
    }


RELAX_WEIGHT = 0.8


def neighbours(padded):
    inner = padded.shape
    result = []
    for dimension in range(3):
        for offset in (0, 2):
            window = [slice(1, -1)] * 3
            window[dimension] = slice(offset, offset + inner[dimension] - 2)
            result.append(tuple(window))
    return result


def stencil(field_pad, coef_pad):
    centre = field_pad[1:-1, 1:-1, 1:-1]
    coef_mid = coef_pad[1:-1, 1:-1, 1:-1]
    total = jnp.zeros(centre.shape, jnp.float32)
    for window in neighbours(field_pad):
        total = total + 0.5 * (coef_mid + coef_pad[window]) * (centre - field_pad[window])
    return total


def diagonal(coef_pad):
    coef_mid = coef_pad[1:-1, 1:-1, 1:-1]
    total = jnp.zeros(coef_mid.shape, jnp.float32)
    for window in neighbours(coef_pad):
        total = total + 0.5 * (coef_mid + coef_pad[window])
    return total


def blocks(field):
    a, b, c = field.shape
    return field.reshape(a // 2, 2, b // 2, 2, c // 2, 2).sum(axis=(1, 3, 5))


def prolong(field):
    return jnp.repeat(jnp.repeat(jnp.repeat(field, 2, axis=0), 2, axis=1), 2, axis=2)


def descend(forcing, coef, depth, start):
    coef_pad = jnp.pad(coef, 1)
    diag_sum = diagonal(coef_pad)
    if start is None:
        guess = RELAX_WEIGHT * forcing / diag_sum
    else:
        guess = start + RELAX_WEIGHT * (forcing - stencil(jnp.pad(start, 1), coef_pad)) / diag_sum
    if depth == LEVELS - 1:
        for sweep in range(COARSE_SWEEPS - 1):
            guess = guess + RELAX_WEIGHT * (forcing - stencil(jnp.pad(guess, 1), coef_pad)) / diag_sum
        residual = forcing - stencil(jnp.pad(guess, 1), coef_pad)
        res_total = jnp.sum(residual, axis=0, keepdims=True)
        diag_total = jnp.sum(diag_sum, axis=0, keepdims=True)
        return guess + RELAX_WEIGHT * res_total / diag_total
    residual = forcing - stencil(jnp.pad(guess, 1), coef_pad)
    coarse = descend(0.5 * blocks(residual), 0.125 * blocks(coef), depth + 1, None)
    guess = guess + prolong(coarse)
    return guess + RELAX_WEIGHT * (forcing - stencil(jnp.pad(guess, 1), coef_pad)) / diag_sum


def reference(source, inv_density, pressure):
    return descend(source, inv_density, 0, pressure)
```

```python
import functools

import jax
import jax.numpy as jnp
from jax import lax
from jax.experimental import pallas as pl
from jax.experimental.pallas import tpu as pltpu
from jax.sharding import PartitionSpec as P

COARSE_SWEEPS = 4
RELAX_WEIGHT = 0.8
KEEP = 1.0 - RELAX_WEIGHT
MESH = pl.DeviceIdType.MESH
CHUNK = 4
SUB = 8

EXCHANGES = ("vin", "b0", "b1", "b2", "v0", "v1", "v2", "u2", "u1", "u0")
LEVEL_OF = {"vin": 0, "b0": 0, "b1": 1, "b2": 2, "v0": 0, "v1": 1, "v2": 2, "u2": 2, "u1": 1, "u0": 0}
SIDES = ("bc", "s0", "s1", "s2", "s3")
GATHERS = ("gb", "gf")


def scratch_plan(depth, lanes, peers):
    plan = {}
    field = lambda planes: pltpu.VMEM((planes * SUB, lanes), jnp.float32)
    for k in range(3):
        z = depth >> k
        for name in ("g", "t", "w", "d", "cym", "cyp", "cxm", "cxp", "ch"):
            plan[name + str(k)] = field(z)
        plan["cz" + str(k)] = field(z + 1)
        for name in ("b", "v", "u"):
            plan[name + str(k)] = field(z + 2)
    plan["vin"] = field(depth + 2)
    for name in EXCHANGES:
        z = depth >> LEVEL_OF[name]
        plan["hx_" + name] = pltpu.VMEM((2, z, lanes), jnp.float32)
        plan["sx_" + name] = pltpu.VMEM((2, z, lanes), jnp.float32)
        plan["hz_" + name] = pltpu.VMEM((2, SUB, lanes), jnp.float32)
    column = 2 * peers
    for name in SIDES:
        plan["hx_" + name] = pltpu.VMEM((2, column, lanes), jnp.float32)
        plan["sx_" + name] = pltpu.VMEM((column, lanes), jnp.float32)
    for name in GATHERS:
        plan["all_" + name] = pltpu.VMEM((peers * SUB, lanes), jnp.float32)
        plan["own_" + name] = pltpu.VMEM((SUB, lanes), jnp.float32)
    plan["r2"] = field(depth >> 2)
    plan["r1"] = field(depth >> 1)
    plan["col"] = pltpu.VMEM((column, lanes), jnp.float32)
    count = 4 * len(EXCHANGES) + 2 * len(SIDES) + (peers - 1) * len(GATHERS)
    plan["send"] = pltpu.SemaphoreType.DMA((count,))
    plan["recv"] = pltpu.SemaphoreType.DMA((count,))
    plan["load"] = pltpu.SemaphoreType.DMA((3,))
    return plan


def cycle_kernel(names, depth, lanes, planes, peers, source, density, pressure, out, *scratch):
    m = dict(zip(names, scratch))
    p, q = lax.axis_index("plane"), lax.axis_index("vert")
    left, right = lax.rem(p + planes - 1, planes), lax.rem(p + 1, planes)
    below, above = lax.rem(q + peers - 1, peers), lax.rem(q + 1, peers)
    p_lo = jnp.where(p == 0, 0.0, 1.0).astype(jnp.float32)
    p_hi = jnp.where(p == planes - 1, 0.0, 1.0).astype(jnp.float32)
    q_lo = jnp.where(q == 0, 0.0, 1.0).astype(jnp.float32)
    q_hi = jnp.where(q == peers - 1, 0.0, 1.0).astype(jnp.float32)

    loads = []
    for i, (src, dst) in enumerate(((density, m["b0"].at[pl.ds(SUB, SUB * depth)]),
                                    (pressure, m["vin"].at[pl.ds(SUB, SUB * depth)]),
                                    (source, m["g0"]))):
        loads.append(pltpu.make_async_copy(src, dst, m["load"].at[i]))
        loads[-1].start()

    barrier = pltpu.get_barrier_semaphore()
    for peer in (left, right):
        pl.semaphore_signal(barrier, inc=1, device_id={"plane": peer}, device_id_type=MESH)
    for step in range(1, peers):
        pl.semaphore_signal(barrier, inc=1, device_id={"vert": lax.rem(q + step, peers)}, device_id_type=MESH)

    zero = jnp.zeros((SUB, lanes), jnp.float32)
    for name in ("vin", "v0", "v1", "v2", "u0", "u1", "u2"):
        z = depth >> LEVEL_OF[name]
        m[name][pl.ds(0, SUB), :] = zero
        m[name][pl.ds(SUB * (z + 1), SUB), :] = zero

    lane = lax.broadcasted_iota(jnp.int32, (SUB, lanes), 1)
    sub = lax.broadcasted_iota(jnp.int32, (SUB, lanes), 0)

    used = [0]
    pending = {}
    started = []

    def remote(key, src, dst, device):
        at = used[0]
        used[0] += 1
        copy = pltpu.make_async_remote_copy(
            src_ref=src, dst_ref=dst, send_sem=m["send"].at[at], recv_sem=m["recv"].at[at],
            device_id=device, device_id_type=MESH)
        copy.start()
        pending.setdefault(key, []).append(copy)
        started.append(copy)

    def arrive(key):
        for copy in pending.pop(key):
            copy.wait_recv()

    def exchange(name, field):
        z = depth >> LEVEL_OF[name]
        hx, sx, hz = m["hx_" + name], m["sx_" + name], m["hz_" + name]
        remote(name, field.at[pl.ds(SUB, SUB)], hz.at[1], {"vert": below})
        remote(name, field.at[pl.ds(SUB * z, SUB)], hz.at[0], {"vert": above})
        for j in range(z):
            sx[0, pl.ds(j, 1), :] = field[pl.ds(SUB * (j + 1), 1), :]
            sx[1, pl.ds(j, 1), :] = field[pl.ds(SUB * (j + 2) - 1, 1), :]
        remote(name, sx.at[0], hx.at[1], {"plane": left})
        remote(name, sx.at[1], hx.at[0], {"plane": right})

    def side(name, value):
        m["sx_" + name][...] = value
        remote(name, m["sx_" + name], m["hx_" + name].at[1], {"plane": left})
        remote(name, m["sx_" + name], m["hx_" + name].at[0], {"plane": right})

    def gather(name, two):
        at = 2 * lax.rem(q, peers // 2)
        tile = jnp.where(sub == at, two[0], jnp.where(sub == at + 1, two[1], 0.0))
        slot = pl.ds(pl.multiple_of(q * SUB, SUB), SUB)
        m["own_" + name][...] = tile
        for step in range(1, peers):
            remote(name, m["own_" + name], m["all_" + name].at[slot], {"vert": lax.rem(q + step, peers)})
        m["all_" + name][slot, :] = tile

    def column(name):
        arrive(name)
        parts = [m["all_" + name][pl.ds(SUB * i, SUB), :] for i in range(peers)]
        half = peers // 2
        return jnp.concatenate([sum(parts[1:half], parts[0]), sum(parts[half + 1:], parts[half])], axis=0)

    def chunks(z, step):
        size = min(CHUNK, z)
        if z == size:
            step(0, size)
        else:
            def run(i, carry):
                step(i * size, size)
                return carry
            lax.fori_loop(0, z // size, run, 0)

    def rows(z, size):
        start = SUB * z
        if not isinstance(z, int):
            start = pl.multiple_of(start, SUB)
        return pl.ds(start, SUB * size)

    def get(name, z, size):
        return m[name][rows(z, size), :].reshape(size, SUB, lanes)

    def put(name, z, size, value):
        m[name][rows(z, size), :] = value.reshape(size * SUB, lanes)

    def restrict(value, k):
        s = 1 << k
        n = value.shape[0]
        value = value.reshape(n // 2, 2, SUB, lanes)
        value = value[:, 0] + value[:, 1]
        value = value + jnp.where((lane & s) != 0, pltpu.roll(value, s, 2), pltpu.roll(value, lanes - s, 2))
        other = pltpu.roll(value, s, 1)
        if 2 * s != SUB:
            other = jnp.where((sub & s) != 0, other, pltpu.roll(value, SUB - s, 1))
        return value + other

    def edge_rows(name, z, size):
        hx = m["hx_" + name]
        result = []
        for j in range(size):
            lo = jnp.broadcast_to(hx[0, pl.ds(z + j, 1), :], (SUB, lanes))
            hi = jnp.broadcast_to(hx[1, pl.ds(z + j, 1), :], (SUB, lanes))
            result.append(jnp.where(sub < SUB // 2, lo, hi))
        return jnp.stack(result)

    def coefficients(k):
        s = 1 << k
        z_all = depth >> k
        name = "b" + str(k)
        arrive(name)
        m[name][rows(0, 1), :] = m["hz_" + name][0] * q_lo
        m[name][rows(z_all + 1, 1), :] = m["hz_" + name][1] * q_hi
        edge = jnp.where(sub < SUB // 2, p_lo, p_hi)
        outer = jnp.logical_or(sub < s, sub >= SUB - s)

        def step(z, size):
            b = 0.5 * get(name, z + 1, size)
            zm = b + 0.5 * get(name, z, size)
            zp = b + 0.5 * get(name, z + 2, size)
            xe = b + 0.5 * (edge_rows(name, z, size) * edge)
            ym_in = jnp.where(lane < s, 0.0, b + pltpu.roll(b, s, 2))
            yp_in = jnp.where(lane >= lanes - s, 0.0, b + pltpu.roll(b, lanes - s, 2))
            xm_in = jnp.where(sub < s, 0.0, b + pltpu.roll(b, s, 1))
            xp_in = jnp.where(sub >= SUB - s, 0.0, b + pltpu.roll(b, SUB - s, 1))
            ch = jnp.where(outer, xe, 0.0)
            ends = jnp.where(jnp.logical_or(lane < s, lane >= lanes - s), b, 0.0)
            diag = zm + zp + ym_in + yp_in + xm_in + xp_in + ch + ends
            k_ = str(k)
            put("cz" + k_, z, size, zm)
            put("cym" + k_, z, size, ym_in)
            put("cyp" + k_, z, size, yp_in)
            put("cxm" + k_, z, size, xm_in)
            put("cxp" + k_, z, size, xp_in)
            put("ch" + k_, z, size, ch * edge)
            put("d" + k_, z, size, diag)
            put("w" + k_, z, size, RELAX_WEIGHT / diag)

        chunks(z_all, step)
        last = 0.5 * m[name][rows(z_all, 1), :] + 0.5 * m[name][rows(z_all + 1, 1), :]
        m["cz" + str(k)][rows(z_all, 1), :] = last * q_hi
        m["cz" + str(k)][rows(0, 1), :] = m["cz" + str(k)][rows(0, 1), :] * q_lo

    def inner_terms(k, name):
        s = 1 << k
        k_ = str(k)

        def step(z, size):
            v = get(name, z + 1, size)
            t = get("g" + k_, z, size)
            t = t + get("cz" + k_, z, size) * get(name, z, size)
            t = t + get("cz" + k_, z + 1, size) * get(name, z + 2, size)
            t = t + get("cym" + k_, z, size) * pltpu.roll(v, s, 2)
            t = t + get("cyp" + k_, z, size) * pltpu.roll(v, lanes - s, 2)
            t = t + get("cxm" + k_, z, size) * pltpu.roll(v, s, 1)
            t = t + get("cxp" + k_, z, size) * pltpu.roll(v, SUB - s, 1)
            put("t" + k_, z, size, t)

        chunks(depth >> k, step)

    def with_halo(k, name, use):
        z_all = depth >> k
        k_ = str(k)
        t, cz, hz = m["t" + k_], m["cz" + k_], m["hz_" + name]
        arrive(name)
        t[rows(0, 1), :] = t[rows(0, 1), :] + cz[rows(0, 1), :] * hz[0]
        t[rows(z_all - 1, 1), :] = t[rows(z_all - 1, 1), :] + cz[rows(z_all, 1), :] * hz[1]

        def step(z, size):
            use(z, size, get("t" + k_, z, size) + get("ch" + k_, z, size) * edge_rows(name, z, size))

        chunks(z_all, step)

    def relaxed(k, name, store):
        k_ = str(k)

        def use(z, size, total):
            store(z, size, KEEP * get(name, z + 1, size) + get("w" + k_, z, size) * total)

        with_halo(k, name, use)

    loads[0].wait()
    loads[1].wait()
    pl.semaphore_wait(barrier, peers + 1)
    exchange("b0", m["b0"])
    exchange("vin", m["vin"])
    for k in range(2):
        def coarser(z, size, k=k):
            half = z // 2
            put("b" + str(k + 1), half + 1, size // 2, 0.125 * restrict(get("b" + str(k), z + 1, size), k))
        chunks(depth >> k, coarser)
        exchange("b" + str(k + 1), m["b" + str(k + 1)])
    gather("gb", 0.125 * restrict(get("b2", 1, depth >> 2), 2))

    coefficients(0)
    loads[2].wait()
    inner_terms(0, "vin")
    relaxed(0, "vin", lambda z, size, value: put("v0", z + 1, size, value))
    exchange("v0", m["v0"])
    inner_terms(0, "v0")
    coefficients(1)
    bc = column("gb")
    side("bc", bc)

    def down(k, name):
        k_, n_ = str(k), str(k + 1)

        def use(z, size, total):
            r = total - get("d" + k_, z, size) * get(name, z + 1, size)
            g = 0.5 * restrict(r, k)
            if k == 2:
                gather("gf", g)
                return
            half = z // 2
            put("g" + n_, half, size // 2, g)
            put("v" + n_, half + 1, size // 2, g * get("w" + n_, half, size // 2))

        with_halo(k, name, use)

    down(0, "v0")
    exchange("v1", m["v1"])
    inner_terms(1, "v1")
    coefficients(2)
    down(1, "v1")
    exchange("v2", m["v2"])
    inner_terms(2, "v2")

    size_y = 1 << 3
    tall = 2 * peers
    lane_c = lax.broadcasted_iota(jnp.int32, (tall, lanes), 1)
    row_c = lax.broadcasted_iota(jnp.int32, (tall, lanes), 0)
    arrive("bc")
    b = 0.5 * bc
    xm = b + (0.5 * p_lo) * m["hx_bc"][0]
    xp = b + (0.5 * p_hi) * m["hx_bc"][1]
    y_lo, y_hi = lane_c < size_y, lane_c >= lanes - size_y
    z_lo, z_hi = row_c == 0, row_c == tall - 1
    ym = b + jnp.where(y_lo, 0.0, pltpu.roll(b, size_y, 1))
    yp = b + jnp.where(y_hi, 0.0, pltpu.roll(b, lanes - size_y, 1))
    zm = b + jnp.where(z_lo, 0.0, pltpu.roll(b, 1, 0))
    zp = b + jnp.where(z_hi, 0.0, pltpu.roll(b, tall - 1, 0))
    diag = xm + xp + ym + yp + zm + zp
    weight = RELAX_WEIGHT / diag
    diag_total = jnp.sum(diag, axis=0, keepdims=True)
    xm, xp = xm * p_lo, xp * p_hi
    ym, yp = jnp.where(y_lo, 0.0, ym), jnp.where(y_hi, 0.0, yp)
    zm, zp = jnp.where(z_lo, 0.0, zm), jnp.where(z_hi, 0.0, zp)

    down(2, "v2")
    forcing = column("gf")
    guess = weight * forcing

    for sweep in range(COARSE_SWEEPS):
        name = "s" + str(sweep)
        side(name, guess)
        total = (forcing + ym * pltpu.roll(guess, size_y, 1) + yp * pltpu.roll(guess, lanes - size_y, 1)
                 + zm * pltpu.roll(guess, 1, 0) + zp * pltpu.roll(guess, tall - 1, 0))
        arrive(name)
        total = total + xm * m["hx_" + name][0] + xp * m["hx_" + name][1]
        if sweep < COARSE_SWEEPS - 1:
            guess = KEEP * guess + weight * total
    res_total = jnp.sum(total - diag * guess, axis=0, keepdims=True)
    m["col"][...] = guess + RELAX_WEIGHT * res_total / diag_total

    own = [jnp.broadcast_to(m["col"][pl.ds(2 * q + j, 1), :], (SUB, lanes)) for j in range(2)]

    for j in range(depth >> 2):
        m["u2"][rows(j + 1, 1), :] = m["v2"][rows(j + 1, 1), :] + own[j // 2]
    exchange("u2", m["u2"])
    inner_terms(2, "u2")
    relaxed(2, "u2", lambda z, size, value: put("r2", z, size, value))

    def add_coarse(k):
        fine, coarse, result = "v" + str(k), "r" + str(k + 1), "u" + str(k)

        def step(z, size):
            half = z // 2
            c = get(coarse, half, size // 2)
            c = jnp.stack([c[i // 2] for i in range(size)])
            put(result, z + 1, size, get(fine, z + 1, size) + c)

        chunks(depth >> k, step)

    add_coarse(1)
    exchange("u1", m["u1"])
    inner_terms(1, "u1")
    relaxed(1, "u1", lambda z, size, value: put("r1", z, size, value))

    add_coarse(0)
    exchange("u0", m["u0"])
    inner_terms(0, "u0")

    def store(z, size, value):
        out[rows(z, size), :] = value.reshape(size * SUB, lanes)

    relaxed(0, "u0", store)
    for copy in started:
        copy.wait_send()


def local(planes, peers, source, density, pressure):
    depth, width, lanes = source.shape
    flat = lambda x: x.reshape(depth * width, lanes)
    plan = scratch_plan(depth, lanes, peers)
    call = pl.pallas_call(
        functools.partial(cycle_kernel, tuple(plan), depth, lanes, planes, peers),
        out_shape=jax.ShapeDtypeStruct((depth * width, lanes), jnp.float32),
        in_specs=[pl.BlockSpec(memory_space=pl.ANY)] * 3,
        out_specs=pl.BlockSpec(memory_space=pltpu.VMEM),
        scratch_shapes=list(plan.values()),
        compiler_params=pltpu.CompilerParams(collective_id=0, has_side_effects=True),
        name="v_cycle",
    )
    return call(flat(source), flat(density), flat(pressure)).reshape(depth, width, lanes)


def solution(mesh):
    spec = P("vert", "plane", None)
    body = functools.partial(local, mesh.shape["plane"], mesh.shape["vert"])
    return jax.shard_map(body, mesh=mesh, in_specs=(spec, spec, spec), out_specs=spec, check_vma=False)
```

```python
import functools

import jax
import jax.numpy as jnp
from jax import lax
from jax.experimental import pallas as pl
from jax.experimental.pallas import tpu as pltpu
from jax.sharding import PartitionSpec as P

COARSE_SWEEPS = 4
RELAX_WEIGHT = 0.8
KEEP = 1.0 - RELAX_WEIGHT
MESH = pl.DeviceIdType.MESH
CHUNK = 4
SUB = 8
NARROW = 128

EXCHANGES = ("vin", "b0", "b1", "b2", "v0", "v1", "v2", "u2", "u1", "u0")
LEVEL_OF = {"vin": 0, "b0": 0, "b1": 1, "b2": 2, "v0": 0, "v1": 1, "v2": 2, "u2": 2, "u1": 1, "u0": 0}
SIDES = {"bc": COARSE_SWEEPS + 1, "fc": COARSE_SWEEPS}
GATHERS = ("gb", "gf")


def scratch_plan(depth, lanes, peers):
    plan = {}
    field = lambda planes: pltpu.VMEM((planes * SUB, lanes), jnp.float32)
    for k in range(3):
        z = depth >> k
        for name in ("g", "t", "w", "d", "cym", "cyp", "cxm", "cxp", "ch"):
            plan[name + str(k)] = field(z)
        plan["cz" + str(k)] = field(z + 1)
        for name in ("b", "v", "u"):
            plan[name + str(k)] = field(z + 2)
    plan["vin"] = field(depth + 2)
    for name in EXCHANGES:
        z = depth >> LEVEL_OF[name]
        plan["hx_" + name] = pltpu.VMEM((2, z, lanes), jnp.float32)
        plan["sx_" + name] = pltpu.VMEM((2, z, lanes), jnp.float32)
        plan["hz_" + name] = pltpu.VMEM((2, SUB, lanes), jnp.float32)
    column = 2 * peers
    for name, reach in SIDES.items():
        plan["hx_" + name] = pltpu.VMEM((2 * reach + 1, column, NARROW), jnp.float32)
        plan["sx_" + name] = pltpu.VMEM((column, NARROW), jnp.float32)
    for name in GATHERS:
        plan["all_" + name] = pltpu.VMEM((peers * SUB, NARROW), jnp.float32)
        plan["own_" + name] = pltpu.VMEM((SUB, NARROW), jnp.float32)
    plan["r2"] = field(depth >> 2)
    plan["r1"] = field(depth >> 1)
    plan["col"] = pltpu.VMEM((column, NARROW), jnp.float32)
    count = 4 * len(EXCHANGES) + 2 * sum(SIDES.values()) + (peers - 1) * len(GATHERS)
    plan["send"] = pltpu.SemaphoreType.DMA((count,))
    plan["recv"] = pltpu.SemaphoreType.DMA((count,))
    plan["load"] = pltpu.SemaphoreType.DMA((3,))
    return plan


def cycle_kernel(names, depth, lanes, planes, peers, source, density, pressure, out, *scratch):
    m = dict(zip(names, scratch))
    p, q = lax.axis_index("plane"), lax.axis_index("vert")
    left, right = lax.rem(p + planes - 1, planes), lax.rem(p + 1, planes)
    below, above = lax.rem(q + peers - 1, peers), lax.rem(q + 1, peers)
    has_left, has_right, has_below, has_above = p > 0, p < planes - 1, q > 0, q < peers - 1
    far = SIDES["bc"]

    loads = []
    for i, (src, dst) in enumerate(((density, m["b0"].at[pl.ds(SUB, SUB * depth)]),
                                    (pressure, m["vin"].at[pl.ds(SUB, SUB * depth)]),
                                    (source, m["g0"]))):
        loads.append(pltpu.make_async_copy(src, dst, m["load"].at[i]))
        loads[-1].start()

    barrier = pltpu.get_barrier_semaphore()
    for step in range(1, far + 1):
        @pl.when(p >= step)
        def _(step=step):
            pl.semaphore_signal(barrier, inc=1, device_id={"plane": p - step}, device_id_type=MESH)

        @pl.when(p + step < planes)
        def _(step=step):
            pl.semaphore_signal(barrier, inc=1, device_id={"plane": p + step}, device_id_type=MESH)
    for step in range(1, peers):
        pl.semaphore_signal(barrier, inc=1, device_id={"vert": lax.rem(q + step, peers)}, device_id_type=MESH)

    zero = jnp.zeros((SUB, lanes), jnp.float32)
    for name in ("vin", "v0", "v1", "v2", "u0", "u1", "u2"):
        z = depth >> LEVEL_OF[name]
        m[name][pl.ds(0, SUB), :] = zero
        m[name][pl.ds(SUB * (z + 1), SUB), :] = zero

    for name in EXCHANGES:
        for absent, half, slot in ((p == 0, "hx_", 0), (p == planes - 1, "hx_", 1),
                                   (q == 0, "hz_", 0), (q == peers - 1, "hz_", 1)):
            @pl.when(absent)
            def _(ref=m[half + name], slot=slot):
                ref[slot] = jnp.zeros(ref.shape[1:], jnp.float32)
    for name, reach in SIDES.items():
        for step in range(1, reach + 1):
            for absent, slot in ((p < step, reach - step), (p + step >= planes, reach + step)):
                @pl.when(absent)
                def _(ref=m["hx_" + name], slot=slot):
                    ref[slot] = jnp.zeros(ref.shape[1:], jnp.float32)

    lane = lax.broadcasted_iota(jnp.int32, (SUB, lanes), 1)
    sub = lax.broadcasted_iota(jnp.int32, (SUB, lanes), 0)

    used = [0]
    pending = {}
    started = []

    def only(condition, action):
        if condition is None:
            action()
        else:
            pl.when(condition)(action)

    def remote(key, src, dst, device, sends=None, receives=None):
        at = used[0]
        used[0] += 1
        copy = pltpu.make_async_remote_copy(
            src_ref=src, dst_ref=dst, send_sem=m["send"].at[at], recv_sem=m["recv"].at[at],
            device_id=device, device_id_type=MESH)
        only(sends, lambda: copy.start())
        pending.setdefault(key, []).append((copy, receives))
        started.append((copy, sends))

    def arrive(key):
        for copy, receives in pending.pop(key):
            only(receives, lambda copy=copy: copy.wait_recv())

    def exchange(name, field):
        z = depth >> LEVEL_OF[name]
        hx, sx, hz = m["hx_" + name], m["sx_" + name], m["hz_" + name]
        remote(name, field.at[pl.ds(SUB, SUB)], hz.at[1], {"vert": below}, has_below, has_above)
        remote(name, field.at[pl.ds(SUB * z, SUB)], hz.at[0], {"vert": above}, has_above, has_below)
        for j in range(z):
            sx[0, pl.ds(j, 1), :] = field[pl.ds(SUB * (j + 1), 1), :]
            sx[1, pl.ds(j, 1), :] = field[pl.ds(SUB * (j + 2) - 1, 1), :]
        remote(name, sx.at[0], hx.at[1], {"plane": left}, has_left, has_right)
        remote(name, sx.at[1], hx.at[0], {"plane": right}, has_right, has_left)

    def side(name, value):
        reach = SIDES[name]
        sx, hx = m["sx_" + name], m["hx_" + name]
        sx[...] = value
        for step in range(1, reach + 1):
            lower, upper = lax.rem(p + planes - step, planes), lax.rem(p + step, planes)
            down, up = p >= step, p + step < planes
            remote(name, sx, hx.at[reach + step], {"plane": lower}, down, up)
            remote(name, sx, hx.at[reach - step], {"plane": upper}, up, down)

    quarter = lax.broadcasted_iota(jnp.int32, (SUB, NARROW), 1) & 3

    def narrow(tile):
        parts = [tile[:, NARROW * j:NARROW * (j + 1)] for j in range(lanes // NARROW)]
        return jnp.where(quarter == 0, parts[0], jnp.where(quarter == 1, parts[1],
                         jnp.where(quarter == 2, parts[2], parts[3])))

    def widen(tile):
        moved = {d: pltpu.roll(tile, (NARROW - d) % NARROW, 1) if d else tile for d in range(-3, 4)}
        return jnp.concatenate(
            [jnp.where(quarter == 0, moved[j], jnp.where(quarter == 1, moved[j - 1],
                       jnp.where(quarter == 2, moved[j - 2], moved[j - 3]))) for j in range(4)], axis=1)

    def gather(name, two):
        at = 2 * lax.rem(q, peers // 2)
        tile = narrow(jnp.where(sub == at, two[0], jnp.where(sub == at + 1, two[1], 0.0)))
        slot = pl.ds(pl.multiple_of(q * SUB, SUB), SUB)
        m["own_" + name][...] = tile
        for step in range(1, peers):
            remote(name, m["own_" + name], m["all_" + name].at[slot], {"vert": lax.rem(q + step, peers)})
        m["all_" + name][slot, :] = tile

    def column(name):
        arrive(name)
        parts = [m["all_" + name][pl.ds(SUB * i, SUB), :] for i in range(peers)]
        half = peers // 2
        return jnp.concatenate([sum(parts[1:half], parts[0]), sum(parts[half + 1:], parts[half])], axis=0)

    def chunks(z, step):
        size = min(CHUNK, z)
        if z == size:
            step(0, size)
        else:
            def run(i, carry):
                step(i * size, size)
                return carry
            lax.fori_loop(0, z // size, run, 0)

    def rows(z, size):
        start = SUB * z
        if not isinstance(z, int):
            start = pl.multiple_of(start, SUB)
        return pl.ds(start, SUB * size)

    def get(name, z, size):
        return m[name][rows(z, size), :].reshape(size, SUB, lanes)

    def put(name, z, size, value):
        m[name][rows(z, size), :] = value.reshape(size * SUB, lanes)

    def restrict(value, k):
        s = 1 << k
        n = value.shape[0]
        value = value.reshape(n // 2, 2, SUB, lanes)
        value = value[:, 0] + value[:, 1]
        value = value + jnp.where((lane & s) != 0, pltpu.roll(value, s, 2), pltpu.roll(value, lanes - s, 2))
        other = pltpu.roll(value, s, 1)
        if 2 * s != SUB:
            other = jnp.where((sub & s) != 0, other, pltpu.roll(value, SUB - s, 1))
        return value + other

    def edge_rows(name, z, size):
        hx = m["hx_" + name]
        result = []
        for j in range(size):
            lo = jnp.broadcast_to(hx[0, pl.ds(z + j, 1), :], (SUB, lanes))
            hi = jnp.broadcast_to(hx[1, pl.ds(z + j, 1), :], (SUB, lanes))
            result.append(jnp.where(sub < SUB // 2, lo, hi))
        return jnp.stack(result)

    def coefficients(k):
        s = 1 << k
        z_all = depth >> k
        name = "b" + str(k)
        arrive(name)
        m[name][rows(0, 1), :] = m["hz_" + name][0]
        m[name][rows(z_all + 1, 1), :] = m["hz_" + name][1]
        outer = jnp.logical_or(sub < s, sub >= SUB - s)

        def step(z, size):
            b = 0.5 * get(name, z + 1, size)
            zm = b + 0.5 * get(name, z, size)
            zp = b + 0.5 * get(name, z + 2, size)
            xe = b + 0.5 * edge_rows(name, z, size)
            ym_in = jnp.where(lane < s, 0.0, b + pltpu.roll(b, s, 2))
            yp_in = jnp.where(lane >= lanes - s, 0.0, b + pltpu.roll(b, lanes - s, 2))
            xm_in = jnp.where(sub < s, 0.0, b + pltpu.roll(b, s, 1))
            xp_in = jnp.where(sub >= SUB - s, 0.0, b + pltpu.roll(b, SUB - s, 1))
            ch = jnp.where(outer, xe, 0.0)
            ends = jnp.where(jnp.logical_or(lane < s, lane >= lanes - s), b, 0.0)
            diag = zm + zp + ym_in + yp_in + xm_in + xp_in + ch + ends
            k_ = str(k)
            put("cz" + k_, z, size, zm)
            put("cym" + k_, z, size, ym_in)
            put("cyp" + k_, z, size, yp_in)
            put("cxm" + k_, z, size, xm_in)
            put("cxp" + k_, z, size, xp_in)
            put("ch" + k_, z, size, ch)
            put("d" + k_, z, size, diag)
            put("w" + k_, z, size, RELAX_WEIGHT / diag)

        chunks(z_all, step)
        last = 0.5 * m[name][rows(z_all, 1), :] + 0.5 * m[name][rows(z_all + 1, 1), :]
        m["cz" + str(k)][rows(z_all, 1), :] = last

    def inner_terms(k, name):
        s = 1 << k
        k_ = str(k)

        def step(z, size):
            v = get(name, z + 1, size)
            t = get("g" + k_, z, size)
            t = t + get("cz" + k_, z, size) * get(name, z, size)
            t = t + get("cz" + k_, z + 1, size) * get(name, z + 2, size)
            t = t + get("cym" + k_, z, size) * pltpu.roll(v, s, 2)
            t = t + get("cyp" + k_, z, size) * pltpu.roll(v, lanes - s, 2)
            t = t + get("cxm" + k_, z, size) * pltpu.roll(v, s, 1)
            t = t + get("cxp" + k_, z, size) * pltpu.roll(v, SUB - s, 1)
            put("t" + k_, z, size, t)

        chunks(depth >> k, step)

    def with_halo(k, name, use):
        z_all = depth >> k
        k_ = str(k)
        t, cz, hz = m["t" + k_], m["cz" + k_], m["hz_" + name]
        arrive(name)
        t[rows(0, 1), :] = t[rows(0, 1), :] + cz[rows(0, 1), :] * hz[0]
        t[rows(z_all - 1, 1), :] = t[rows(z_all - 1, 1), :] + cz[rows(z_all, 1), :] * hz[1]

        def step(z, size):
            use(z, size, get("t" + k_, z, size) + get("ch" + k_, z, size) * edge_rows(name, z, size))

        chunks(z_all, step)

    def relaxed(k, name, store):
        k_ = str(k)

        def use(z, size, total):
            store(z, size, KEEP * get(name, z + 1, size) + get("w" + k_, z, size) * total)

        with_halo(k, name, use)

    loads[0].wait()
    loads[1].wait()
    greeted = jnp.minimum(p, far) + jnp.minimum(planes - 1 - p, far) + peers - 1
    pl.semaphore_wait(barrier, greeted)
    exchange("b0", m["b0"])
    exchange("vin", m["vin"])
    for k in range(2):
        def coarser(z, size, k=k):
            half = z // 2
            put("b" + str(k + 1), half + 1, size // 2, 0.125 * restrict(get("b" + str(k), z + 1, size), k))
        chunks(depth >> k, coarser)
        exchange("b" + str(k + 1), m["b" + str(k + 1)])
    gather("gb", 0.125 * restrict(get("b2", 1, depth >> 2), 2))

    coefficients(0)
    loads[2].wait()
    inner_terms(0, "vin")
    relaxed(0, "vin", lambda z, size, value: put("v0", z + 1, size, value))
    exchange("v0", m["v0"])
    inner_terms(0, "v0")
    coefficients(1)
    bc = column("gb")
    side("bc", bc)

    def down(k, name):
        k_, n_ = str(k), str(k + 1)

        def use(z, size, total):
            r = total - get("d" + k_, z, size) * get(name, z + 1, size)
            g = 0.5 * restrict(r, k)
            if k == 2:
                gather("gf", g)
                return
            half = z // 2
            put("g" + n_, half, size // 2, g)
            put("v" + n_, half + 1, size // 2, g * get("w" + n_, half, size // 2))

        with_halo(k, name, use)

    down(0, "v0")
    exchange("v1", m["v1"])
    inner_terms(1, "v1")
    coefficients(2)
    down(1, "v1")
    exchange("v2", m["v2"])
    inner_terms(2, "v2")

    reach = COARSE_SWEEPS
    tall = 2 * peers
    lane_c = lax.broadcasted_iota(jnp.int32, (tall, NARROW), 1)
    row_c = lax.broadcasted_iota(jnp.int32, (tall, NARROW), 0)
    y_lo = jnp.logical_or(lane_c == 0, lane_c == 4)
    y_hi = jnp.logical_or(lane_c == NARROW - 5, lane_c == NARROW - 1)
    z_lo, z_hi = row_c == 0, row_c == tall - 1

    def before_y(v):
        return jnp.where(lane_c < 8, pltpu.roll(v, 9, 1), pltpu.roll(v, 8, 1))

    def after_y(v):
        return jnp.where(lane_c >= NARROW - 8, pltpu.roll(v, NARROW - 9, 1), pltpu.roll(v, NARROW - 8, 1))

    arrive("bc")
    b = {o: 0.5 * (bc if o == 0 else m["hx_bc"][far + o]) for o in range(-far, far + 1)}
    xp = {o: b[o] + b[o + 1] for o in range(-far, far)}
    ym, yp, zm, zp, weight = {}, {}, {}, {}, {}
    for o in range(-reach, reach + 1):
        ym[o] = b[o] + jnp.where(y_lo, 0.0, before_y(b[o]))
        yp[o] = b[o] + jnp.where(y_hi, 0.0, after_y(b[o]))
        zm[o] = b[o] + jnp.where(z_lo, 0.0, pltpu.roll(b[o], 1, 0))
        zp[o] = b[o] + jnp.where(z_hi, 0.0, pltpu.roll(b[o], tall - 1, 0))
        diag = xp[o - 1] + xp[o] + ym[o] + yp[o] + zm[o] + zp[o]
        if o == 0:
            diag_own = diag
            weight[o] = RELAX_WEIGHT / diag
        else:
            inside = jnp.where(jnp.logical_and(p + o >= 0, p + o < planes), 1.0, 0.0).astype(jnp.float32)
            weight[o] = (RELAX_WEIGHT * inside) / (diag + (1.0 - inside))
        ym[o], yp[o] = jnp.where(y_lo, 0.0, ym[o]), jnp.where(y_hi, 0.0, yp[o])
        zm[o], zp[o] = jnp.where(z_lo, 0.0, zm[o]), jnp.where(z_hi, 0.0, zp[o])
    diag_total = jnp.sum(diag_own, axis=0, keepdims=True)

    down(2, "v2")
    own_forcing = column("gf")
    side("fc", own_forcing)
    arrive("fc")
    forcing = {o: own_forcing if o == 0 else m["hx_fc"][reach + o] for o in range(-reach, reach + 1)}
    guess = {o: weight[o] * forcing[o] for o in forcing}

    def total_of(o):
        v = guess[o]
        return (forcing[o] + xp[o - 1] * guess[o - 1] + xp[o] * guess[o + 1]
                + ym[o] * before_y(v) + yp[o] * after_y(v)
                + zm[o] * pltpu.roll(v, 1, 0) + zp[o] * pltpu.roll(v, tall - 1, 0))

    for wide in range(COARSE_SWEEPS - 1, 0, -1):
        guess = {o: KEEP * guess[o] + weight[o] * total_of(o) for o in range(-wide, wide + 1)}
    res_total = jnp.sum(total_of(0) - diag_own * guess[0], axis=0, keepdims=True)
    m["col"][...] = guess[0] + RELAX_WEIGHT * res_total / diag_total

    own = [widen(jnp.broadcast_to(m["col"][pl.ds(2 * q + j, 1), :], (SUB, NARROW))) for j in range(2)]

    for j in range(depth >> 2):
        m["u2"][rows(j + 1, 1), :] = m["v2"][rows(j + 1, 1), :] + own[j // 2]
    exchange("u2", m["u2"])
    inner_terms(2, "u2")
    relaxed(2, "u2", lambda z, size, value: put("r2", z, size, value))

    def add_coarse(k):
        fine, coarse, result = "v" + str(k), "r" + str(k + 1), "u" + str(k)

        def step(z, size):
            half = z // 2
            c = get(coarse, half, size // 2)
            c = jnp.stack([c[i // 2] for i in range(size)])
            put(result, z + 1, size, get(fine, z + 1, size) + c)

        chunks(depth >> k, step)

    add_coarse(1)
    exchange("u1", m["u1"])
    inner_terms(1, "u1")
    relaxed(1, "u1", lambda z, size, value: put("r1", z, size, value))

    add_coarse(0)
    exchange("u0", m["u0"])
    inner_terms(0, "u0")

    def store(z, size, value):
        out[rows(z, size), :] = value.reshape(size * SUB, lanes)

    relaxed(0, "u0", store)
    for copy, sends in started:
        only(sends, lambda copy=copy: copy.wait_send())


def local(planes, peers, source, density, pressure):
    depth, width, lanes = source.shape
    flat = lambda x: x.reshape(depth * width, lanes)
    plan = scratch_plan(depth, lanes, peers)
    call = pl.pallas_call(
        functools.partial(cycle_kernel, tuple(plan), depth, lanes, planes, peers),
        out_shape=jax.ShapeDtypeStruct((depth * width, lanes), jnp.float32),
        in_specs=[pl.BlockSpec(memory_space=pl.ANY)] * 3,
        out_specs=pl.BlockSpec(memory_space=pltpu.VMEM),
        scratch_shapes=list(plan.values()),
        compiler_params=pltpu.CompilerParams(collective_id=0, has_side_effects=True),
        name="v_cycle",
    )
    return call(flat(source), flat(density), flat(pressure)).reshape(depth, width, lanes)


def solution(mesh):
    spec = P("vert", "plane", None)
    body = functools.partial(local, mesh.shape["plane"], mesh.shape["vert"])
    return jax.shard_map(body, mesh=mesh, in_specs=(spec, spec, spec), out_specs=spec, check_vma=False)
```

```python
import functools

import jax
import jax.numpy as jnp
from jax import lax
from jax.experimental import pallas as pl
from jax.experimental.pallas import tpu as pltpu
from jax.sharding import PartitionSpec as P

COARSE_SWEEPS = 4
RELAX_WEIGHT = 0.8
KEEP = 1.0 - RELAX_WEIGHT
MESH = pl.DeviceIdType.MESH
CHUNK = 4
SUB = 8
NARROW = 128

EXCHANGES = ("vin", "b0", "b1", "b2", "v0", "v1", "v2", "u2", "u1", "u0")
LEVEL_OF = {"vin": 0, "b0": 0, "b1": 1, "b2": 2, "v0": 0, "v1": 1, "v2": 2, "u2": 2, "u1": 1, "u0": 0}
SIDES = {"bc": COARSE_SWEEPS + 2, "fc": COARSE_SWEEPS + 1}
GATHERS = ("gb", "gf")


def scratch_plan(depth, lanes, peers):
    plan = {}
    field = lambda planes: pltpu.VMEM((planes * SUB, lanes), jnp.float32)
    for k in range(3):
        z = depth >> k
        for name in ("g", "t", "w", "d", "cym", "cyp", "cxm", "cxp", "ch"):
            plan[name + str(k)] = field(z)
        plan["cz" + str(k)] = field(z + 1)
        for name in ("b", "v", "u"):
            plan[name + str(k)] = field(z + 2)
    plan["vin"] = field(depth + 2)
    for name in EXCHANGES:
        z = depth >> LEVEL_OF[name]
        plan["hx_" + name] = pltpu.VMEM((2, z, lanes), jnp.float32)
        plan["sx_" + name] = pltpu.VMEM((2, z, lanes), jnp.float32)
        plan["hz_" + name] = pltpu.VMEM((2, SUB, lanes), jnp.float32)
    column = 2 * peers
    for name, reach in SIDES.items():
        plan["hx_" + name] = pltpu.VMEM((2 * reach + 1, column, NARROW), jnp.float32)
        plan["sx_" + name] = pltpu.VMEM((column, NARROW), jnp.float32)
    for name in GATHERS:
        plan["all_" + name] = pltpu.VMEM((peers * SUB, NARROW), jnp.float32)
        plan["own_" + name] = pltpu.VMEM((SUB, NARROW), jnp.float32)
    plan["r2"] = field(depth >> 2)
    plan["r1"] = field(depth >> 1)
    plan["col"] = pltpu.VMEM((3, column + 2 * SUB, NARROW), jnp.float32)
    plan["pick"] = pltpu.VMEM((SUB, NARROW), jnp.float32)
    plan["wide"] = pltpu.VMEM((SUB, lanes), jnp.float32)
    count = 4 * len(EXCHANGES) + 2 * sum(SIDES.values()) + (peers - 1) * len(GATHERS)
    plan["send"] = pltpu.SemaphoreType.DMA((count,))
    plan["recv"] = pltpu.SemaphoreType.DMA((count,))
    plan["load"] = pltpu.SemaphoreType.DMA((3,))
    return plan


def cycle_kernel(names, depth, lanes, planes, peers, source, density, pressure, out, *scratch):
    m = dict(zip(names, scratch))
    p, q = lax.axis_index("plane"), lax.axis_index("vert")
    left, right = lax.rem(p + planes - 1, planes), lax.rem(p + 1, planes)
    below, above = lax.rem(q + peers - 1, peers), lax.rem(q + 1, peers)
    has_left, has_right, has_below, has_above = p > 0, p < planes - 1, q > 0, q < peers - 1
    far = SIDES["bc"]

    loads = []
    for i, (src, dst) in enumerate(((density, m["b0"].at[pl.ds(SUB, SUB * depth)]),
                                    (pressure, m["vin"].at[pl.ds(SUB, SUB * depth)]),
                                    (source, m["g0"]))):
        loads.append(pltpu.make_async_copy(src, dst, m["load"].at[i]))
        loads[-1].start()

    barrier = pltpu.get_barrier_semaphore()
    for step in range(1, far + 1):
        @pl.when(p >= step)
        def _(step=step):
            pl.semaphore_signal(barrier, inc=1, device_id={"plane": p - step}, device_id_type=MESH)

        @pl.when(p + step < planes)
        def _(step=step):
            pl.semaphore_signal(barrier, inc=1, device_id={"plane": p + step}, device_id_type=MESH)
    for step in range(1, peers):
        pl.semaphore_signal(barrier, inc=1, device_id={"vert": lax.rem(q + step, peers)}, device_id_type=MESH)

    zero = jnp.zeros((SUB, lanes), jnp.float32)
    for name in ("vin", "v0", "v1", "v2", "u0", "u1", "u2"):
        z = depth >> LEVEL_OF[name]
        m[name][pl.ds(0, SUB), :] = zero
        m[name][pl.ds(SUB * (z + 1), SUB), :] = zero

    for name in EXCHANGES:
        for absent, half, slot in ((p == 0, "hx_", 0), (p == planes - 1, "hx_", 1),
                                   (q == 0, "hz_", 0), (q == peers - 1, "hz_", 1)):
            @pl.when(absent)
            def _(ref=m[half + name], slot=slot):
                ref[slot] = jnp.zeros(ref.shape[1:], jnp.float32)
    for name, reach in SIDES.items():
        for step in range(1, reach + 1):
            for absent, slot in ((p < step, reach - step), (p + step >= planes, reach + step)):
                @pl.when(absent)
                def _(ref=m["hx_" + name], slot=slot):
                    ref[slot] = jnp.zeros(ref.shape[1:], jnp.float32)

    lane = lax.broadcasted_iota(jnp.int32, (SUB, lanes), 1)
    sub = lax.broadcasted_iota(jnp.int32, (SUB, lanes), 0)

    used = [0]
    pending = {}
    started = []

    def only(condition, action):
        if condition is None:
            action()
        else:
            pl.when(condition)(action)

    def remote(key, src, dst, device, sends=None, receives=None):
        at = used[0]
        used[0] += 1
        copy = pltpu.make_async_remote_copy(
            src_ref=src, dst_ref=dst, send_sem=m["send"].at[at], recv_sem=m["recv"].at[at],
            device_id=device, device_id_type=MESH)
        only(sends, lambda: copy.start())
        pending.setdefault(key, []).append((copy, receives))
        started.append((copy, sends))

    def arrive(key):
        for copy, receives in pending.pop(key, ()):
            only(receives, lambda copy=copy: copy.wait_recv())

    def exchange(name, field):
        z = depth >> LEVEL_OF[name]
        hx, sx, hz = m["hx_" + name], m["sx_" + name], m["hz_" + name]
        for j in range(z):
            sx[0, pl.ds(j, 1), :] = field[pl.ds(SUB * (j + 1), 1), :]
            sx[1, pl.ds(j, 1), :] = field[pl.ds(SUB * (j + 2) - 1, 1), :]
        remote(name, sx.at[0], hx.at[1], {"plane": left}, has_left, has_right)
        remote(name, sx.at[1], hx.at[0], {"plane": right}, has_right, has_left)
        remote(name, field.at[pl.ds(SUB, SUB)], hz.at[1], {"vert": below}, has_below, has_above)
        remote(name, field.at[pl.ds(SUB * z, SUB)], hz.at[0], {"vert": above}, has_above, has_below)

    def side(name, value):
        reach = SIDES[name]
        sx, hx = m["sx_" + name], m["hx_" + name]
        sx[...] = value
        for step in range(1, reach + 1):
            lower, upper = lax.rem(p + planes - step, planes), lax.rem(p + step, planes)
            down, up = p >= step, p + step < planes
            remote(name, sx, hx.at[reach + step], {"plane": lower}, down, up)
            remote(name, sx, hx.at[reach - step], {"plane": upper}, up, down)

    quarter = lax.broadcasted_iota(jnp.int32, (SUB, NARROW), 1) & 3

    def narrow(tile):
        parts = [tile[:, NARROW * j:NARROW * (j + 1)] for j in range(lanes // NARROW)]
        return jnp.where(quarter == 0, parts[0], jnp.where(quarter == 1, parts[1],
                         jnp.where(quarter == 2, parts[2], parts[3])))

    def widen(tile):
        moved = {d: pltpu.roll(tile, (NARROW - d) % NARROW, 1) if d else tile for d in range(-3, 4)}
        return jnp.concatenate(
            [jnp.where(quarter == 0, moved[j], jnp.where(quarter == 1, moved[j - 1],
                       jnp.where(quarter == 2, moved[j - 2], moved[j - 3]))) for j in range(4)], axis=1)

    def gather(name, two):
        at = 2 * lax.rem(q, peers // 2)
        tile = narrow(jnp.where(sub == at, two[0], jnp.where(sub == at + 1, two[1], 0.0)))
        slot = pl.ds(pl.multiple_of(q * SUB, SUB), SUB)
        m["own_" + name][...] = tile
        for step in range(1, peers):
            remote(name, m["own_" + name], m["all_" + name].at[slot], {"vert": lax.rem(q + step, peers)})
        m["all_" + name][slot, :] = tile

    def column(name):
        arrive(name)
        parts = [m["all_" + name][pl.ds(SUB * i, SUB), :] for i in range(peers)]
        half = peers // 2
        return jnp.concatenate([sum(parts[1:half], parts[0]), sum(parts[half + 1:], parts[half])], axis=0)

    def chunks(z, step):
        size = min(CHUNK, z)
        if z == size:
            step(0, size)
        else:
            def run(i, carry):
                step(i * size, size)
                return carry
            lax.fori_loop(0, z // size, run, 0, unroll=True)

    def rows(z, size):
        start = SUB * z
        if not isinstance(z, int):
            start = pl.multiple_of(start, SUB)
        return pl.ds(start, SUB * size)

    def get(name, z, size):
        return m[name][rows(z, size), :].reshape(size, SUB, lanes)

    def put(name, z, size, value):
        m[name][rows(z, size), :] = value.reshape(size * SUB, lanes)

    def restrict(value, k):
        s = 1 << k
        n = value.shape[0]
        value = value.reshape(n // 2, 2, SUB, lanes)
        value = value[:, 0] + value[:, 1]
        value = value + jnp.where((lane & s) != 0, pltpu.roll(value, s, 2), pltpu.roll(value, lanes - s, 2))
        other = pltpu.roll(value, s, 1)
        if 2 * s != SUB:
            other = jnp.where((sub & s) != 0, other, pltpu.roll(value, SUB - s, 1))
        return value + other

    def edge_rows(name, z, size):
        hx = m["hx_" + name]
        result = []
        for j in range(size):
            lo = jnp.broadcast_to(hx[0, pl.ds(z + j, 1), :], (SUB, lanes))
            hi = jnp.broadcast_to(hx[1, pl.ds(z + j, 1), :], (SUB, lanes))
            result.append(jnp.where(sub < SUB // 2, lo, hi))
        return jnp.stack(result)

    def coefficients(k):
        s = 1 << k
        z_all = depth >> k
        name = "b" + str(k)
        arrive(name)
        m[name][rows(0, 1), :] = m["hz_" + name][0]
        m[name][rows(z_all + 1, 1), :] = m["hz_" + name][1]
        outer = jnp.logical_or(sub < s, sub >= SUB - s)

        def step(z, size):
            b = 0.5 * get(name, z + 1, size)
            zm = b + 0.5 * get(name, z, size)
            zp = b + 0.5 * get(name, z + 2, size)
            xe = b + 0.5 * edge_rows(name, z, size)
            ym_in = jnp.where(lane < s, 0.0, b + pltpu.roll(b, s, 2))
            yp_in = jnp.where(lane >= lanes - s, 0.0, b + pltpu.roll(b, lanes - s, 2))
            xm_in = jnp.where(sub < s, 0.0, b + pltpu.roll(b, s, 1))
            xp_in = jnp.where(sub >= SUB - s, 0.0, b + pltpu.roll(b, SUB - s, 1))
            ch = jnp.where(outer, xe, 0.0)
            ends = jnp.where(jnp.logical_or(lane < s, lane >= lanes - s), b, 0.0)
            diag = zm + zp + ym_in + yp_in + xm_in + xp_in + ch + ends
            k_ = str(k)
            put("cz" + k_, z, size, zm)
            put("cym" + k_, z, size, ym_in)
            put("cyp" + k_, z, size, yp_in)
            put("cxm" + k_, z, size, xm_in)
            put("cxp" + k_, z, size, xp_in)
            put("ch" + k_, z, size, ch)
            put("d" + k_, z, size, diag)
            put("w" + k_, z, size, RELAX_WEIGHT / diag)

        chunks(z_all, step)
        last = 0.5 * m[name][rows(z_all, 1), :] + 0.5 * m[name][rows(z_all + 1, 1), :]
        m["cz" + str(k)][rows(z_all, 1), :] = last

    def inner_terms(k, name):
        s = 1 << k
        k_ = str(k)

        def step(z, size):
            v = get(name, z + 1, size)
            t = get("g" + k_, z, size)
            t = t + get("cz" + k_, z, size) * get(name, z, size)
            t = t + get("cz" + k_, z + 1, size) * get(name, z + 2, size)
            t = t + get("cym" + k_, z, size) * pltpu.roll(v, s, 2)
            t = t + get("cyp" + k_, z, size) * pltpu.roll(v, lanes - s, 2)
            t = t + get("cxm" + k_, z, size) * pltpu.roll(v, s, 1)
            t = t + get("cxp" + k_, z, size) * pltpu.roll(v, SUB - s, 1)
            put("t" + k_, z, size, t)

        chunks(depth >> k, step)

    def with_halo(k, name, use):
        z_all = depth >> k
        k_ = str(k)
        t, cz, hz = m["t" + k_], m["cz" + k_], m["hz_" + name]
        arrive(name)
        t[rows(0, 1), :] = t[rows(0, 1), :] + cz[rows(0, 1), :] * hz[0]
        t[rows(z_all - 1, 1), :] = t[rows(z_all - 1, 1), :] + cz[rows(z_all, 1), :] * hz[1]

        def step(z, size):
            use(z, size, get("t" + k_, z, size) + get("ch" + k_, z, size) * edge_rows(name, z, size))

        chunks(z_all, step)

    def relaxed(k, name, store):
        k_ = str(k)

        def use(z, size, total):
            store(z, size, KEEP * get(name, z + 1, size) + get("w" + k_, z, size) * total)

        with_halo(k, name, use)

    loads[0].wait()
    loads[1].wait()
    greeted = jnp.minimum(p, far) + jnp.minimum(planes - 1 - p, far) + peers - 1
    pl.semaphore_wait(barrier, greeted)
    exchange("b0", m["b0"])
    exchange("vin", m["vin"])
    for k in range(2):
        def coarser(z, size, k=k):
            half = z // 2
            put("b" + str(k + 1), half + 1, size // 2, 0.125 * restrict(get("b" + str(k), z + 1, size), k))
        chunks(depth >> k, coarser)
        exchange("b" + str(k + 1), m["b" + str(k + 1)])
    gather("gb", 0.125 * restrict(get("b2", 1, depth >> 2), 2))

    coefficients(0)
    loads[2].wait()
    inner_terms(0, "vin")
    relaxed(0, "vin", lambda z, size, value: put("v0", z + 1, size, value))
    exchange("v0", m["v0"])
    inner_terms(0, "v0")
    coefficients(1)
    bc = column("gb")
    side("bc", bc)

    def down(k, name):
        k_, n_ = str(k), str(k + 1)

        def use(z, size, total):
            r = total - get("d" + k_, z, size) * get(name, z + 1, size)
            g = 0.5 * restrict(r, k)
            if k == 2:
                gather("gf", g)
                return
            half = z // 2
            put("g" + n_, half, size // 2, g)
            put("v" + n_, half + 1, size // 2, g * get("w" + n_, half, size // 2))

        with_halo(k, name, use)

    down(0, "v0")
    exchange("v1", m["v1"])
    inner_terms(1, "v1")
    coefficients(2)
    down(1, "v1")
    exchange("v2", m["v2"])
    inner_terms(2, "v2")

    reach = COARSE_SWEEPS + 1
    tall = 2 * peers
    lane_c = lax.broadcasted_iota(jnp.int32, (tall, NARROW), 1)
    row_c = lax.broadcasted_iota(jnp.int32, (tall, NARROW), 0)
    y_lo = jnp.logical_or(lane_c == 0, lane_c == 4)
    y_hi = jnp.logical_or(lane_c == NARROW - 5, lane_c == NARROW - 1)
    z_lo, z_hi = row_c == 0, row_c == tall - 1

    def before_y(v):
        return jnp.where(lane_c < 8, pltpu.roll(v, 9, 1), pltpu.roll(v, 8, 1))

    def after_y(v):
        return jnp.where(lane_c >= NARROW - 8, pltpu.roll(v, NARROW - 9, 1), pltpu.roll(v, NARROW - 8, 1))

    arrive("bc")
    b = {o: 0.5 * (bc if o == 0 else m["hx_bc"][far + o]) for o in range(-far, far + 1)}
    xp = {o: b[o] + b[o + 1] for o in range(-far, far)}
    ym, yp, zm, zp, diag, weight, inside = {}, {}, {}, {}, {}, {}, {}
    for o in range(-reach, reach + 1):
        ym[o] = b[o] + jnp.where(y_lo, 0.0, before_y(b[o]))
        yp[o] = b[o] + jnp.where(y_hi, 0.0, after_y(b[o]))
        zm[o] = b[o] + jnp.where(z_lo, 0.0, pltpu.roll(b[o], 1, 0))
        zp[o] = b[o] + jnp.where(z_hi, 0.0, pltpu.roll(b[o], tall - 1, 0))
        diag[o] = xp[o - 1] + xp[o] + ym[o] + yp[o] + zm[o] + zp[o]
        inside[o] = jnp.where(jnp.logical_and(p + o >= 0, p + o < planes), 1.0, 0.0).astype(jnp.float32)
        weight[o] = (RELAX_WEIGHT * inside[o]) / (diag[o] + (1.0 - inside[o]))
        ym[o], yp[o] = jnp.where(y_lo, 0.0, ym[o]), jnp.where(y_hi, 0.0, yp[o])
        zm[o], zp[o] = jnp.where(z_lo, 0.0, zm[o]), jnp.where(z_hi, 0.0, zp[o])
    share = {o: RELAX_WEIGHT * inside[o] / (jnp.sum(diag[o], axis=0, keepdims=True) + (1.0 - inside[o]))
             for o in (-1, 0, 1)}
    for o in range(3):
        m["col"][o, pl.ds(0, SUB), :] = jnp.zeros((SUB, NARROW), jnp.float32)
        m["col"][o, pl.ds(SUB + tall, SUB), :] = jnp.zeros((SUB, NARROW), jnp.float32)

    down(2, "v2")
    own_forcing = column("gf")
    side("fc", own_forcing)
    arrive("fc")
    forcing = {o: own_forcing if o == 0 else m["hx_fc"][reach + o] for o in range(-reach, reach + 1)}
    guess = {o: weight[o] * forcing[o] for o in forcing}

    def total_of(o):
        v = guess[o]
        return (forcing[o] + xp[o - 1] * guess[o - 1] + xp[o] * guess[o + 1]
                + ym[o] * before_y(v) + yp[o] * after_y(v)
                + zm[o] * pltpu.roll(v, 1, 0) + zp[o] * pltpu.roll(v, tall - 1, 0))

    for wide in range(COARSE_SWEEPS, 1, -1):
        guess = {o: KEEP * guess[o] + weight[o] * total_of(o) for o in range(-wide, wide + 1)}
    for o in (-1, 0, 1):
        res_total = jnp.sum(total_of(o) - diag[o] * guess[o], axis=0, keepdims=True)
        m["col"][o + 1, pl.ds(SUB, tall), :] = guess[o] + share[o] * res_total

    for i, (o, j) in enumerate(((0, -1), (0, 0), (0, 1), (0, 2), (-1, 0), (-1, 1), (1, 0), (1, 1))):
        m["pick"][pl.ds(i, 1), :] = m["col"][o + 1, pl.ds(SUB + 2 * q + j, 1), :]
    m["wide"][...] = widen(m["pick"][...])

    def under(i):
        return m["wide"][pl.ds(i, 1), :]

    spread = lambda row: jnp.broadcast_to(row, (SUB, lanes))
    for j in range(depth >> 2):
        m["u2"][rows(j + 1, 1), :] = m["v2"][rows(j + 1, 1), :] + spread(under(1 + j // 2))
        m["hx_u2"][0, pl.ds(j, 1), :] = m["hx_v2"][0, pl.ds(j, 1), :] + under(4 + j // 2)
        m["hx_u2"][1, pl.ds(j, 1), :] = m["hx_v2"][1, pl.ds(j, 1), :] + under(6 + j // 2)
    m["hz_u2"][0] = m["hz_v2"][0] + spread(under(0))
    m["hz_u2"][1] = m["hz_v2"][1] + spread(under(3))
    inner_terms(2, "u2")
    relaxed(2, "u2", lambda z, size, value: put("r2", z, size, value))

    def add_coarse(k):
        fine, coarse, result = "v" + str(k), "r" + str(k + 1), "u" + str(k)

        def step(z, size):
            half = z // 2
            c = get(coarse, half, size // 2)
            c = jnp.stack([c[i // 2] for i in range(size)])
            put(result, z + 1, size, get(fine, z + 1, size) + c)

        chunks(depth >> k, step)

    add_coarse(1)
    exchange("u1", m["u1"])
    inner_terms(1, "u1")
    relaxed(1, "u1", lambda z, size, value: put("r1", z, size, value))

    add_coarse(0)
    exchange("u0", m["u0"])
    inner_terms(0, "u0")

    def store(z, size, value):
        out[rows(z, size), :] = value.reshape(size * SUB, lanes)

    relaxed(0, "u0", store)
    for copy, sends in started:
        only(sends, lambda copy=copy: copy.wait_send())


def local(planes, peers, source, density, pressure):
    depth, width, lanes = source.shape
    flat = lambda x: x.reshape(depth * width, lanes)
    plan = scratch_plan(depth, lanes, peers)
    call = pl.pallas_call(
        functools.partial(cycle_kernel, tuple(plan), depth, lanes, planes, peers),
        out_shape=jax.ShapeDtypeStruct((depth * width, lanes), jnp.float32),
        in_specs=[pl.BlockSpec(memory_space=pl.ANY)] * 3,
        out_specs=pl.BlockSpec(memory_space=pltpu.VMEM),
        scratch_shapes=list(plan.values()),
        compiler_params=pltpu.CompilerParams(collective_id=0, has_side_effects=True),
        name="v_cycle",
    )
    return call(flat(source), flat(density), flat(pressure)).reshape(depth, width, lanes)


def solution(mesh):
    spec = P("vert", "plane", None)
    body = functools.partial(local, mesh.shape["plane"], mesh.shape["vert"])
    return jax.shard_map(body, mesh=mesh, in_specs=(spec, spec, spec), out_specs=spec, check_vma=False)
```

```python
import functools

import jax
import jax.numpy as jnp
from jax import lax
from jax.experimental import pallas as pl
from jax.experimental.pallas import tpu as pltpu
from jax.sharding import PartitionSpec as P

COARSE_SWEEPS = 4
RELAX_WEIGHT = 0.8
KEEP = 1.0 - RELAX_WEIGHT
MESH = pl.DeviceIdType.MESH
CHUNK = 4
SUB = 8
NARROW = 128

EXCHANGES = ("vin", "b0", "b1", "b2", "v0", "v1", "v2", "u2", "u1", "u0")
LEVEL_OF = {"vin": 0, "b0": 0, "b1": 1, "b2": 2, "v0": 0, "v1": 1, "v2": 2, "u2": 2, "u1": 1, "u0": 0}
SIDES = {"bc": COARSE_SWEEPS + 2, "fc": COARSE_SWEEPS + 1}
GATHERS = ("gb", "gf")


def scratch_plan(depth, lanes, peers):
    plan = {}
    field = lambda planes: pltpu.VMEM((planes * SUB, lanes), jnp.float32)
    for k in range(3):
        z = depth >> k
        for name in ("g", "t", "w", "d", "cym", "cyp", "cxm", "cxp", "ch"):
            plan[name + str(k)] = field(z)
        plan["cz" + str(k)] = field(z + 1)
        for name in ("b", "v", "u"):
            plan[name + str(k)] = field(z + 2)
    plan["vin"] = field(depth + 2)
    for name in EXCHANGES:
        z = depth >> LEVEL_OF[name]
        plan["hx_" + name] = pltpu.VMEM((2, z, lanes), jnp.float32)
        plan["sx_" + name] = pltpu.VMEM((2, z, lanes), jnp.float32)
        plan["hz_" + name] = pltpu.VMEM((2, SUB, lanes), jnp.float32)
    column = 2 * peers
    for name, reach in SIDES.items():
        plan["hx_" + name] = pltpu.VMEM((2 * reach + 1, SUB, NARROW), jnp.float32)
        plan["sx_" + name] = pltpu.VMEM((SUB, NARROW), jnp.float32)
    for name in GATHERS:
        plan["all_" + name] = pltpu.VMEM((peers * SUB, NARROW), jnp.float32)
        plan["own_" + name] = pltpu.VMEM((SUB, NARROW), jnp.float32)
    plan["r2"] = field(depth >> 2)
    plan["r1"] = field(depth >> 1)
    plan["col"] = pltpu.VMEM((3, column + 2 * SUB, NARROW), jnp.float32)
    plan["pick"] = pltpu.VMEM((SUB, NARROW), jnp.float32)
    plan["wide"] = pltpu.VMEM((SUB, lanes), jnp.float32)
    count = 4 * len(EXCHANGES) + 2 * sum(SIDES.values()) + (peers - 1) * len(GATHERS)
    plan["send"] = pltpu.SemaphoreType.DMA((count,))
    plan["recv"] = pltpu.SemaphoreType.DMA((count,))
    plan["load"] = pltpu.SemaphoreType.DMA((3,))
    return plan


def cycle_kernel(names, depth, lanes, planes, peers, source, density, pressure, out, *scratch):
    m = dict(zip(names, scratch))
    p, q = lax.axis_index("plane"), lax.axis_index("vert")
    left, right = lax.rem(p + planes - 1, planes), lax.rem(p + 1, planes)
    below, above = lax.rem(q + peers - 1, peers), lax.rem(q + 1, peers)
    has_left, has_right, has_below, has_above = p > 0, p < planes - 1, q > 0, q < peers - 1
    far = SIDES["bc"]

    loads = []
    for i, (src, dst) in enumerate(((density, m["b0"].at[pl.ds(SUB, SUB * depth)]),
                                    (pressure, m["vin"].at[pl.ds(SUB, SUB * depth)]),
                                    (source, m["g0"]))):
        loads.append(pltpu.make_async_copy(src, dst, m["load"].at[i]))
        loads[-1].start()

    barrier = pltpu.get_barrier_semaphore()
    for step in range(1, far + 1):
        @pl.when(p >= step)
        def _(step=step):
            pl.semaphore_signal(barrier, inc=1, device_id={"plane": p - step}, device_id_type=MESH)

        @pl.when(p + step < planes)
        def _(step=step):
            pl.semaphore_signal(barrier, inc=1, device_id={"plane": p + step}, device_id_type=MESH)
    for step in range(1, peers):
        pl.semaphore_signal(barrier, inc=1, device_id={"vert": lax.rem(q + step, peers)}, device_id_type=MESH)

    zero = jnp.zeros((SUB, lanes), jnp.float32)
    for name in ("vin", "v0", "v1", "v2", "u0", "u1", "u2", "b0", "b1", "b2"):
        z = depth >> LEVEL_OF[name]
        m[name][pl.ds(0, SUB), :] = zero
        m[name][pl.ds(SUB * (z + 1), SUB), :] = zero

    for name in EXCHANGES:
        for absent, half, slot in ((p == 0, "hx_", 0), (p == planes - 1, "hx_", 1),
                                   (q == 0, "hz_", 0), (q == peers - 1, "hz_", 1)):
            @pl.when(absent)
            def _(ref=m[half + name], slot=slot):
                ref[slot] = jnp.zeros(ref.shape[1:], jnp.float32)
    for name, reach in SIDES.items():
        for step in range(1, reach + 1):
            for absent, slot in ((p < step, reach - step), (p + step >= planes, reach + step)):
                @pl.when(absent)
                def _(ref=m["hx_" + name], slot=slot):
                    ref[slot] = jnp.zeros(ref.shape[1:], jnp.float32)

    lane = lax.broadcasted_iota(jnp.int32, (SUB, lanes), 1)
    sub = lax.broadcasted_iota(jnp.int32, (SUB, lanes), 0)

    used = [0]
    pending = {}
    started = []

    def only(condition, action):
        if condition is None:
            action()
        else:
            pl.when(condition)(action)

    def remote(key, src, dst, device, sends=None, receives=None):
        at = used[0]
        used[0] += 1
        copy = pltpu.make_async_remote_copy(
            src_ref=src, dst_ref=dst, send_sem=m["send"].at[at], recv_sem=m["recv"].at[at],
            device_id=device, device_id_type=MESH)
        only(sends, lambda: copy.start())
        pending.setdefault(key, []).append((copy, receives))
        started.append((copy, sends))

    def arrive(key):
        for copy, receives in pending.pop(key, ()):
            only(receives, lambda copy=copy: copy.wait_recv())

    def exchange(name, field):
        z = depth >> LEVEL_OF[name]
        hx, sx, hz = m["hx_" + name], m["sx_" + name], m["hz_" + name]
        for j in range(z):
            sx[0, pl.ds(j, 1), :] = field[pl.ds(SUB * (j + 1), 1), :]
            sx[1, pl.ds(j, 1), :] = field[pl.ds(SUB * (j + 2) - 1, 1), :]
        remote(name, sx.at[0], hx.at[1], {"plane": left}, has_left, has_right)
        remote(name, sx.at[1], hx.at[0], {"plane": right}, has_right, has_left)
        remote(name, field.at[pl.ds(SUB, SUB)], hz.at[1], {"vert": below}, has_below, has_above)
        remote(name, field.at[pl.ds(SUB * z, SUB)], hz.at[0], {"vert": above}, has_above, has_below)

    def side(name, value):
        reach = SIDES[name]
        sx, hx = m["sx_" + name], m["hx_" + name]
        sx[...] = jnp.where(twin, value[SUB:], value[:SUB])
        for step in range(1, reach + 1):
            lower, upper = lax.rem(p + planes - step, planes), lax.rem(p + step, planes)
            down, up = p >= step, p + step < planes
            remote(name, sx, hx.at[reach + step], {"plane": lower}, down, up)
            remote(name, sx, hx.at[reach - step], {"plane": upper}, up, down)

    quarter = lax.broadcasted_iota(jnp.int32, (SUB, NARROW), 1) & 3

    twin = (lax.broadcasted_iota(jnp.int32, (SUB, NARROW), 1) & 4) != 0

    def side_column(name, offset):
        both = m["hx_" + name][SIDES[name] + offset]
        top = jnp.where(twin, pltpu.roll(both, 4, 1), both)
        return jnp.concatenate([top, jnp.where(twin, both, pltpu.roll(both, NARROW - 4, 1))], axis=0)

    def narrow(tile):
        parts = [tile[:, NARROW * j:NARROW * (j + 1)] for j in range(lanes // NARROW)]
        return jnp.where(quarter == 0, parts[0], jnp.where(quarter == 1, parts[1],
                         jnp.where(quarter == 2, parts[2], parts[3])))

    def widen(tile):
        moved = {d: pltpu.roll(tile, (NARROW - d) % NARROW, 1) if d else tile for d in range(-3, 4)}
        return jnp.concatenate(
            [jnp.where(quarter == 0, moved[j], jnp.where(quarter == 1, moved[j - 1],
                       jnp.where(quarter == 2, moved[j - 2], moved[j - 3]))) for j in range(4)], axis=1)

    def gather(name, two):
        at = 2 * lax.rem(q, peers // 2)
        tile = narrow(jnp.where(sub == at, two[0], jnp.where(sub == at + 1, two[1], 0.0)))
        slot = pl.ds(pl.multiple_of(q * SUB, SUB), SUB)
        m["own_" + name][...] = tile
        for step in range(1, peers):
            remote(name, m["own_" + name], m["all_" + name].at[slot], {"vert": lax.rem(q + step, peers)})
        m["all_" + name][slot, :] = tile

    def column(name):
        arrive(name)
        parts = [m["all_" + name][pl.ds(SUB * i, SUB), :] for i in range(peers)]
        half = peers // 2
        return jnp.concatenate([sum(parts[1:half], parts[0]), sum(parts[half + 1:], parts[half])], axis=0)

    def chunks(z, step):
        size = min(CHUNK, z)
        if z == size:
            step(0, size)
        else:
            def run(i, carry):
                step(i * size, size)
                return carry
            lax.fori_loop(0, z // size, run, 0, unroll=True)

    def rows(z, size):
        start = SUB * z
        if not isinstance(z, int):
            start = pl.multiple_of(start, SUB)
        return pl.ds(start, SUB * size)

    def get(name, z, size):
        return m[name][rows(z, size), :].reshape(size, SUB, lanes)

    def put(name, z, size, value):
        m[name][rows(z, size), :] = value.reshape(size * SUB, lanes)

    def restrict(value, k):
        s = 1 << k
        n = value.shape[0]
        value = value.reshape(n // 2, 2, SUB, lanes)
        value = value[:, 0] + value[:, 1]
        value = value + jnp.where((lane & s) != 0, pltpu.roll(value, s, 2), pltpu.roll(value, lanes - s, 2))
        other = pltpu.roll(value, s, 1)
        if 2 * s != SUB:
            other = jnp.where((sub & s) != 0, other, pltpu.roll(value, SUB - s, 1))
        return value + other

    def edge_rows(name, z, size):
        hx = m["hx_" + name]
        result = []
        for j in range(size):
            lo = jnp.broadcast_to(hx[0, pl.ds(z + j, 1), :], (SUB, lanes))
            hi = jnp.broadcast_to(hx[1, pl.ds(z + j, 1), :], (SUB, lanes))
            result.append(jnp.where(sub < SUB // 2, lo, hi))
        return jnp.stack(result)

    def inner_coefficients(k):
        s = 1 << k
        z_all = depth >> k
        name, k_ = "b" + str(k), str(k)
        ends_y = jnp.logical_or(lane < s, lane >= lanes - s)

        def step(z, size):
            b = 0.5 * get(name, z + 1, size)
            zm = b + 0.5 * get(name, z, size)
            zp = b + 0.5 * get(name, z + 2, size)
            ym = jnp.where(lane < s, 0.0, b + pltpu.roll(b, s, 2))
            yp = jnp.where(lane >= lanes - s, 0.0, b + pltpu.roll(b, lanes - s, 2))
            xm = jnp.where(sub < s, 0.0, b + pltpu.roll(b, s, 1))
            xp = jnp.where(sub >= SUB - s, 0.0, b + pltpu.roll(b, SUB - s, 1))
            put("cz" + k_, z, size, zm)
            put("cym" + k_, z, size, ym)
            put("cyp" + k_, z, size, yp)
            put("cxm" + k_, z, size, xm)
            put("cxp" + k_, z, size, xp)
            put("d" + k_, z, size, zm + zp + ym + yp + xm + xp + jnp.where(ends_y, b, 0.0))

        chunks(z_all, step)
        m["cz" + k_][rows(z_all, 1), :] = 0.5 * m[name][rows(z_all, 1), :]

    def finish_coefficients(k):
        s = 1 << k
        z_all = depth >> k
        name, k_ = "b" + str(k), str(k)
        cz, d, hz = m["cz" + k_], m["d" + k_], m["hz_" + name]
        outer = jnp.logical_or(sub < s, sub >= SUB - s)
        arrive(name)
        lo, hi = 0.5 * hz[0], 0.5 * hz[1]
        cz[rows(0, 1), :] = cz[rows(0, 1), :] + lo
        cz[rows(z_all, 1), :] = cz[rows(z_all, 1), :] + hi
        d[rows(0, 1), :] = d[rows(0, 1), :] + lo
        d[rows(z_all - 1, 1), :] = d[rows(z_all - 1, 1), :] + hi

        def step(z, size):
            ch = jnp.where(outer, 0.5 * (get(name, z + 1, size) + edge_rows(name, z, size)), 0.0)
            diag = get("d" + k_, z, size) + ch
            put("ch" + k_, z, size, ch)
            put("d" + k_, z, size, diag)
            put("w" + k_, z, size, RELAX_WEIGHT / diag)

        chunks(z_all, step)

    def inner_terms(k, name):
        s = 1 << k
        k_ = str(k)

        def step(z, size):
            v = get(name, z + 1, size)
            t = get("g" + k_, z, size)
            t = t + get("cz" + k_, z, size) * get(name, z, size)
            t = t + get("cz" + k_, z + 1, size) * get(name, z + 2, size)
            t = t + get("cym" + k_, z, size) * pltpu.roll(v, s, 2)
            t = t + get("cyp" + k_, z, size) * pltpu.roll(v, lanes - s, 2)
            t = t + get("cxm" + k_, z, size) * pltpu.roll(v, s, 1)
            t = t + get("cxp" + k_, z, size) * pltpu.roll(v, SUB - s, 1)
            put("t" + k_, z, size, t)

        chunks(depth >> k, step)

    def with_halo(k, name, use):
        z_all = depth >> k
        k_ = str(k)
        t, cz, hz = m["t" + k_], m["cz" + k_], m["hz_" + name]
        arrive(name)
        t[rows(0, 1), :] = t[rows(0, 1), :] + cz[rows(0, 1), :] * hz[0]
        t[rows(z_all - 1, 1), :] = t[rows(z_all - 1, 1), :] + cz[rows(z_all, 1), :] * hz[1]

        def step(z, size):
            use(z, size, get("t" + k_, z, size) + get("ch" + k_, z, size) * edge_rows(name, z, size))

        chunks(z_all, step)

    def relaxed(k, name, store):
        k_ = str(k)

        def use(z, size, total):
            store(z, size, KEEP * get(name, z + 1, size) + get("w" + k_, z, size) * total)

        with_halo(k, name, use)

    loads[0].wait()
    loads[1].wait()
    greeted = jnp.minimum(p, far) + jnp.minimum(planes - 1 - p, far) + peers - 1
    pl.semaphore_wait(barrier, greeted)
    exchange("b0", m["b0"])
    exchange("vin", m["vin"])
    for k in range(2):
        def coarser(z, size, k=k):
            half = z // 2
            put("b" + str(k + 1), half + 1, size // 2, 0.125 * restrict(get("b" + str(k), z + 1, size), k))
        chunks(depth >> k, coarser)
        exchange("b" + str(k + 1), m["b" + str(k + 1)])
    gather("gb", 0.125 * restrict(get("b2", 1, depth >> 2), 2))

    inner_coefficients(0)
    loads[2].wait()
    inner_terms(0, "vin")
    finish_coefficients(0)
    relaxed(0, "vin", lambda z, size, value: put("v0", z + 1, size, value))
    exchange("v0", m["v0"])
    inner_terms(0, "v0")
    inner_coefficients(1)
    finish_coefficients(1)
    bc = column("gb")
    side("bc", bc)

    def down(k, name):
        k_, n_ = str(k), str(k + 1)

        def use(z, size, total):
            r = total - get("d" + k_, z, size) * get(name, z + 1, size)
            g = 0.5 * restrict(r, k)
            if k == 2:
                gather("gf", g)
                return
            half = z // 2
            put("g" + n_, half, size // 2, g)
            put("v" + n_, half + 1, size // 2, g * get("w" + n_, half, size // 2))

        with_halo(k, name, use)

    down(0, "v0")
    exchange("v1", m["v1"])
    inner_terms(1, "v1")
    inner_coefficients(2)
    finish_coefficients(2)
    down(1, "v1")
    exchange("v2", m["v2"])
    inner_terms(2, "v2")

    reach = COARSE_SWEEPS + 1
    tall = 2 * peers
    lane_c = lax.broadcasted_iota(jnp.int32, (tall, NARROW), 1)
    row_c = lax.broadcasted_iota(jnp.int32, (tall, NARROW), 0)
    y_lo = jnp.logical_or(lane_c == 0, lane_c == 4)
    y_hi = jnp.logical_or(lane_c == NARROW - 5, lane_c == NARROW - 1)
    z_lo, z_hi = row_c == 0, row_c == tall - 1

    def before_y(v):
        return jnp.where(lane_c < 8, pltpu.roll(v, 9, 1), pltpu.roll(v, 8, 1))

    def after_y(v):
        return jnp.where(lane_c >= NARROW - 8, pltpu.roll(v, NARROW - 9, 1), pltpu.roll(v, NARROW - 8, 1))

    arrive("bc")
    b = {o: 0.5 * (bc if o == 0 else side_column("bc", o)) for o in range(-far, far + 1)}
    xp = {o: b[o] + b[o + 1] for o in range(-far, far)}
    ym, yp, zm, zp, diag, weight, inside = {}, {}, {}, {}, {}, {}, {}
    for o in range(-reach, reach + 1):
        ym[o] = b[o] + jnp.where(y_lo, 0.0, before_y(b[o]))
        yp[o] = b[o] + jnp.where(y_hi, 0.0, after_y(b[o]))
        zm[o] = b[o] + jnp.where(z_lo, 0.0, pltpu.roll(b[o], 1, 0))
        zp[o] = b[o] + jnp.where(z_hi, 0.0, pltpu.roll(b[o], tall - 1, 0))
        diag[o] = xp[o - 1] + xp[o] + ym[o] + yp[o] + zm[o] + zp[o]
        inside[o] = jnp.where(jnp.logical_and(p + o >= 0, p + o < planes), 1.0, 0.0).astype(jnp.float32)
        weight[o] = (RELAX_WEIGHT * inside[o]) / (diag[o] + (1.0 - inside[o]))
        ym[o], yp[o] = jnp.where(y_lo, 0.0, ym[o]), jnp.where(y_hi, 0.0, yp[o])
        zm[o], zp[o] = jnp.where(z_lo, 0.0, zm[o]), jnp.where(z_hi, 0.0, zp[o])
    share = {o: RELAX_WEIGHT * inside[o] / (jnp.sum(diag[o], axis=0, keepdims=True) + (1.0 - inside[o]))
             for o in (-1, 0, 1)}
    for o in range(3):
        m["col"][o, pl.ds(0, SUB), :] = jnp.zeros((SUB, NARROW), jnp.float32)
        m["col"][o, pl.ds(SUB + tall, SUB), :] = jnp.zeros((SUB, NARROW), jnp.float32)

    down(2, "v2")
    own_forcing = column("gf")
    side("fc", own_forcing)
    arrive("fc")
    forcing = {o: own_forcing if o == 0 else side_column("fc", o) for o in range(-reach, reach + 1)}
    guess = {o: weight[o] * forcing[o] for o in forcing}

    def total_of(o):
        v = guess[o]
        return (forcing[o] + xp[o - 1] * guess[o - 1] + xp[o] * guess[o + 1]
                + ym[o] * before_y(v) + yp[o] * after_y(v)
                + zm[o] * pltpu.roll(v, 1, 0) + zp[o] * pltpu.roll(v, tall - 1, 0))

    for wide in range(COARSE_SWEEPS, 1, -1):
        guess = {o: KEEP * guess[o] + weight[o] * total_of(o) for o in range(-wide, wide + 1)}
    for o in (-1, 0, 1):
        res_total = jnp.sum(total_of(o) - diag[o] * guess[o], axis=0, keepdims=True)
        m["col"][o + 1, pl.ds(SUB, tall), :] = guess[o] + share[o] * res_total

    for i, (o, j) in enumerate(((0, -1), (0, 0), (0, 1), (0, 2), (-1, 0), (-1, 1), (1, 0), (1, 1))):
        m["pick"][pl.ds(i, 1), :] = m["col"][o + 1, pl.ds(SUB + 2 * q + j, 1), :]
    m["wide"][...] = widen(m["pick"][...])

    def under(i):
        return m["wide"][pl.ds(i, 1), :]

    spread = lambda row: jnp.broadcast_to(row, (SUB, lanes))
    for j in range(depth >> 2):
        m["u2"][rows(j + 1, 1), :] = m["v2"][rows(j + 1, 1), :] + spread(under(1 + j // 2))
        m["hx_u2"][0, pl.ds(j, 1), :] = m["hx_v2"][0, pl.ds(j, 1), :] + under(4 + j // 2)
        m["hx_u2"][1, pl.ds(j, 1), :] = m["hx_v2"][1, pl.ds(j, 1), :] + under(6 + j // 2)
    m["hz_u2"][0] = m["hz_v2"][0] + spread(under(0))
    m["hz_u2"][1] = m["hz_v2"][1] + spread(under(3))
    inner_terms(2, "u2")
    relaxed(2, "u2", lambda z, size, value: put("r2", z, size, value))

    def add_coarse(k):
        fine, coarse, result = "v" + str(k), "r" + str(k + 1), "u" + str(k)

        def step(z, size):
            half = z // 2
            c = get(coarse, half, size // 2)
            c = jnp.stack([c[i // 2] for i in range(size)])
            put(result, z + 1, size, get(fine, z + 1, size) + c)

        chunks(depth >> k, step)

    add_coarse(1)
    exchange("u1", m["u1"])
    inner_terms(1, "u1")
    relaxed(1, "u1", lambda z, size, value: put("r1", z, size, value))

    add_coarse(0)
    exchange("u0", m["u0"])
    inner_terms(0, "u0")

    def store(z, size, value):
        out[rows(z, size), :] = value.reshape(size * SUB, lanes)

    relaxed(0, "u0", store)
    for copy, sends in started:
        only(sends, lambda copy=copy: copy.wait_send())


def local(planes, peers, source, density, pressure):
    depth, width, lanes = source.shape
    flat = lambda x: x.reshape(depth * width, lanes)
    plan = scratch_plan(depth, lanes, peers)
    call = pl.pallas_call(
        functools.partial(cycle_kernel, tuple(plan), depth, lanes, planes, peers),
        out_shape=jax.ShapeDtypeStruct((depth * width, lanes), jnp.float32),
        in_specs=[pl.BlockSpec(memory_space=pl.ANY)] * 3,
        out_specs=pl.BlockSpec(memory_space=pltpu.VMEM),
        scratch_shapes=list(plan.values()),
        compiler_params=pltpu.CompilerParams(collective_id=0, has_side_effects=True),
        name="v_cycle",
    )
    return call(flat(source), flat(density), flat(pressure)).reshape(depth, width, lanes)


def solution(mesh):
    spec = P("vert", "plane", None)
    body = functools.partial(local, mesh.shape["plane"], mesh.shape["vert"])
    return jax.shard_map(body, mesh=mesh, in_specs=(spec, spec, spec), out_specs=spec, check_vma=False)
```

```python
import functools

import jax
import jax.numpy as jnp
from jax import lax
from jax.experimental import pallas as pl
from jax.experimental.pallas import tpu as pltpu
from jax.sharding import PartitionSpec as P

COARSE_SWEEPS = 4
RELAX_WEIGHT = 0.8
KEEP = 1.0 - RELAX_WEIGHT
MESH = pl.DeviceIdType.MESH
CHUNK = 8
SUB = 8
NARROW = 128
GRANT = 56170000

EXCHANGES = ("vin", "b0", "b1", "b2", "v0", "v1", "v2", "u2", "r2", "r1")
LEVEL_OF = {"vin": 0, "b0": 0, "b1": 1, "b2": 2, "v0": 0, "v1": 1, "v2": 2, "u2": 2, "u1": 1, "u0": 0, "r2": 2, "r1": 1}
SIDES = {"bc": COARSE_SWEEPS + 2, "fc": COARSE_SWEEPS + 1}
GATHERS = ("gb", "gf")


def scratch_plan(depth, lanes, peers):
    plan = {}
    field = lambda planes: pltpu.VMEM((planes * SUB, lanes), jnp.float32)
    for k in range(3):
        z = depth >> k
        for name in ("g", "t", "w", "d", "cym", "cyp", "cxm", "cxp", "ch"):
            plan[name + str(k)] = field(z)
        plan["cz" + str(k)] = field(z + 1)
        for name in ("b", "v", "u"):
            plan[name + str(k)] = field(z + 2)
    plan["vin"] = field(depth + 2)
    for name in EXCHANGES:
        z = depth >> LEVEL_OF[name]
        plan["hx_" + name] = pltpu.VMEM((2, z, lanes), jnp.float32)
        plan["sx_" + name] = pltpu.VMEM((2, z, lanes), jnp.float32)
        plan["hz_" + name] = pltpu.VMEM((2, SUB, lanes), jnp.float32)
    column = 2 * peers
    for name, reach in SIDES.items():
        plan["hx_" + name] = pltpu.VMEM((2 * reach + 1, SUB, NARROW), jnp.float32)
        plan["sx_" + name] = pltpu.VMEM((SUB, NARROW), jnp.float32)
    for name in GATHERS:
        plan["all_" + name] = pltpu.VMEM((peers * SUB, NARROW), jnp.float32)
        plan["own_" + name] = pltpu.VMEM((SUB, NARROW), jnp.float32)
    plan["r2"] = field((depth >> 2) + 2)
    plan["r1"] = field((depth >> 1) + 2)
    plan["col"] = pltpu.VMEM((3, column + 2 * SUB, NARROW), jnp.float32)
    plan["pick"] = pltpu.VMEM((SUB, NARROW), jnp.float32)
    plan["wide"] = pltpu.VMEM((SUB, lanes), jnp.float32)
    count = 4 * len(EXCHANGES) + 2 * sum(SIDES.values()) + (peers - 1) * len(GATHERS)
    plan["send"] = pltpu.SemaphoreType.DMA((count,))
    plan["recv"] = pltpu.SemaphoreType.DMA((count,))
    plan["load"] = pltpu.SemaphoreType.DMA((3,))
    return plan


def cycle_kernel(names, depth, lanes, planes, peers, source, density, pressure, out, *scratch):
    m = dict(zip(names, scratch))
    p, q = lax.axis_index("plane"), lax.axis_index("vert")
    left, right = lax.rem(p + planes - 1, planes), lax.rem(p + 1, planes)
    below, above = lax.rem(q + peers - 1, peers), lax.rem(q + 1, peers)
    has_left, has_right, has_below, has_above = p > 0, p < planes - 1, q > 0, q < peers - 1
    far = SIDES["bc"]

    loads = []
    for i, (src, dst) in enumerate(((density, m["b0"].at[pl.ds(SUB, SUB * depth)]),
                                    (pressure, m["vin"].at[pl.ds(SUB, SUB * depth)]),
                                    (source, m["g0"]))):
        loads.append(pltpu.make_async_copy(src, dst, m["load"].at[i]))
        loads[-1].start()

    barrier = pltpu.get_barrier_semaphore()
    for step in range(1, far + 1):
        @pl.when(p >= step)
        def _(step=step):
            pl.semaphore_signal(barrier, inc=1, device_id={"plane": p - step}, device_id_type=MESH)

        @pl.when(p + step < planes)
        def _(step=step):
            pl.semaphore_signal(barrier, inc=1, device_id={"plane": p + step}, device_id_type=MESH)
    for step in range(1, peers):
        pl.semaphore_signal(barrier, inc=1, device_id={"vert": lax.rem(q + step, peers)}, device_id_type=MESH)

    zero = jnp.zeros((SUB, lanes), jnp.float32)
    for name in ("vin", "v0", "v1", "v2", "u0", "u1", "u2", "b0", "b1", "b2"):
        z = depth >> LEVEL_OF[name]
        m[name][pl.ds(0, SUB), :] = zero
        m[name][pl.ds(SUB * (z + 1), SUB), :] = zero

    for name in EXCHANGES:
        for absent, half, slot in ((p == 0, "hx_", 0), (p == planes - 1, "hx_", 1),
                                   (q == 0, "hz_", 0), (q == peers - 1, "hz_", 1)):
            @pl.when(absent)
            def _(ref=m[half + name], slot=slot):
                ref[slot] = jnp.zeros(ref.shape[1:], jnp.float32)
    for name, reach in SIDES.items():
        for step in range(1, reach + 1):
            for absent, slot in ((p < step, reach - step), (p + step >= planes, reach + step)):
                @pl.when(absent)
                def _(ref=m["hx_" + name], slot=slot):
                    ref[slot] = jnp.zeros(ref.shape[1:], jnp.float32)

    lane = lax.broadcasted_iota(jnp.int32, (SUB, lanes), 1)
    sub = lax.broadcasted_iota(jnp.int32, (SUB, lanes), 0)

    used = [0]
    pending = {}
    started = []

    def only(condition, action):
        if condition is None:
            action()
        else:
            pl.when(condition)(action)

    def remote(key, src, dst, device, sends=None, receives=None):
        at = used[0]
        used[0] += 1
        copy = pltpu.make_async_remote_copy(
            src_ref=src, dst_ref=dst, send_sem=m["send"].at[at], recv_sem=m["recv"].at[at],
            device_id=device, device_id_type=MESH)
        only(sends, lambda: copy.start())
        pending.setdefault(key, []).append((copy, receives))
        started.append((copy, sends))

    def arrive(key):
        for copy, receives in pending.pop(key, ()):
            only(receives, lambda copy=copy: copy.wait_recv())

    def exchange(name, field):
        z = depth >> LEVEL_OF[name]
        hx, sx, hz = m["hx_" + name], m["sx_" + name], m["hz_" + name]
        for j in range(z):
            sx[0, pl.ds(j, 1), :] = field[pl.ds(SUB * (j + 1), 1), :]
            sx[1, pl.ds(j, 1), :] = field[pl.ds(SUB * (j + 2) - 1, 1), :]
        remote(name, sx.at[0], hx.at[1], {"plane": left}, has_left, has_right)
        remote(name, sx.at[1], hx.at[0], {"plane": right}, has_right, has_left)
        remote(name, field.at[pl.ds(SUB, SUB)], hz.at[1], {"vert": below}, has_below, has_above)
        remote(name, field.at[pl.ds(SUB * z, SUB)], hz.at[0], {"vert": above}, has_above, has_below)

    def side(name, value):
        reach = SIDES[name]
        sx, hx = m["sx_" + name], m["hx_" + name]
        sx[...] = jnp.where(twin, value[SUB:], value[:SUB])
        for step in range(1, reach + 1):
            lower, upper = lax.rem(p + planes - step, planes), lax.rem(p + step, planes)
            down, up = p >= step, p + step < planes
            remote(name, sx, hx.at[reach + step], {"plane": lower}, down, up)
            remote(name, sx, hx.at[reach - step], {"plane": upper}, up, down)

    quarter = lax.broadcasted_iota(jnp.int32, (SUB, NARROW), 1) & 3

    twin = (lax.broadcasted_iota(jnp.int32, (SUB, NARROW), 1) & 4) != 0

    def side_column(name, offset):
        both = m["hx_" + name][SIDES[name] + offset]
        top = jnp.where(twin, pltpu.roll(both, 4, 1), both)
        return jnp.concatenate([top, jnp.where(twin, both, pltpu.roll(both, NARROW - 4, 1))], axis=0)

    def narrow(tile):
        parts = [tile[:, NARROW * j:NARROW * (j + 1)] for j in range(lanes // NARROW)]
        return jnp.where(quarter == 0, parts[0], jnp.where(quarter == 1, parts[1],
                         jnp.where(quarter == 2, parts[2], parts[3])))

    def widen(tile):
        moved = {d: pltpu.roll(tile, (NARROW - d) % NARROW, 1) if d else tile for d in range(-3, 4)}
        return jnp.concatenate(
            [jnp.where(quarter == 0, moved[j], jnp.where(quarter == 1, moved[j - 1],
                       jnp.where(quarter == 2, moved[j - 2], moved[j - 3]))) for j in range(4)], axis=1)

    def gather(name, two):
        at = 2 * lax.rem(q, peers // 2)
        tile = narrow(jnp.where(sub == at, two[0], jnp.where(sub == at + 1, two[1], 0.0)))
        slot = pl.ds(pl.multiple_of(q * SUB, SUB), SUB)
        m["own_" + name][...] = tile
        for step in range(1, peers):
            remote(name, m["own_" + name], m["all_" + name].at[slot], {"vert": lax.rem(q + step, peers)})
        m["all_" + name][slot, :] = tile

    def column(name):
        arrive(name)
        parts = [m["all_" + name][pl.ds(SUB * i, SUB), :] for i in range(peers)]
        half = peers // 2
        return jnp.concatenate([sum(parts[1:half], parts[0]), sum(parts[half + 1:], parts[half])], axis=0)

    def chunks(z, step):
        size = min(CHUNK, z)
        if z == size:
            step(0, size)
        else:
            def run(i, carry):
                step(i * size, size)
                return carry
            lax.fori_loop(0, z // size, run, 0, unroll=True)

    def rows(z, size):
        start = SUB * z
        if not isinstance(z, int):
            start = pl.multiple_of(start, SUB)
        return pl.ds(start, SUB * size)

    def get(name, z, size):
        return m[name][rows(z, size), :].reshape(size, SUB, lanes)

    def put(name, z, size, value):
        m[name][rows(z, size), :] = value.reshape(size * SUB, lanes)

    def restrict(value, k):
        s = 1 << k
        n = value.shape[0]
        value = value.reshape(n // 2, 2, SUB, lanes)
        value = value[:, 0] + value[:, 1]
        value = value + jnp.where((lane & s) != 0, pltpu.roll(value, s, 2), pltpu.roll(value, lanes - s, 2))
        other = pltpu.roll(value, s, 1)
        if 2 * s != SUB:
            other = jnp.where((sub & s) != 0, other, pltpu.roll(value, SUB - s, 1))
        return value + other

    def edge_rows(name, z, size, coarse=None):
        hx = m["hx_" + name]
        result = []
        for j in range(size):
            lo, hi = hx[0, pl.ds(z + j, 1), :], hx[1, pl.ds(z + j, 1), :]
            if coarse is not None:
                below_it = pl.ds(z // 2 + j // 2, 1)
                lo, hi = lo + m["hx_" + coarse][0, below_it, :], hi + m["hx_" + coarse][1, below_it, :]
            lo, hi = jnp.broadcast_to(lo, (SUB, lanes)), jnp.broadcast_to(hi, (SUB, lanes))
            result.append(jnp.where(sub < SUB // 2, lo, hi))
        return jnp.stack(result)

    def inner_coefficients(k):
        s = 1 << k
        z_all = depth >> k
        name, k_ = "b" + str(k), str(k)
        ends_y = jnp.logical_or(lane < s, lane >= lanes - s)

        def step(z, size):
            b = 0.5 * get(name, z + 1, size)
            zm = b + 0.5 * get(name, z, size)
            zp = b + 0.5 * get(name, z + 2, size)
            ym = jnp.where(lane < s, 0.0, b + pltpu.roll(b, s, 2))
            yp = jnp.where(lane >= lanes - s, 0.0, b + pltpu.roll(b, lanes - s, 2))
            xm = jnp.where(sub < s, 0.0, b + pltpu.roll(b, s, 1))
            xp = jnp.where(sub >= SUB - s, 0.0, b + pltpu.roll(b, SUB - s, 1))
            put("cz" + k_, z, size, zm)
            put("cym" + k_, z, size, ym)
            put("cyp" + k_, z, size, yp)
            put("cxm" + k_, z, size, xm)
            put("cxp" + k_, z, size, xp)
            put("d" + k_, z, size, zm + zp + ym + yp + xm + xp + jnp.where(ends_y, b, 0.0))

        chunks(z_all, step)
        m["cz" + k_][rows(z_all, 1), :] = 0.5 * m[name][rows(z_all, 1), :]

    def finish_coefficients(k):
        s = 1 << k
        z_all = depth >> k
        name, k_ = "b" + str(k), str(k)
        cz, d, hz = m["cz" + k_], m["d" + k_], m["hz_" + name]
        outer = jnp.logical_or(sub < s, sub >= SUB - s)
        arrive(name)
        lo, hi = 0.5 * hz[0], 0.5 * hz[1]
        cz[rows(0, 1), :] = cz[rows(0, 1), :] + lo
        cz[rows(z_all, 1), :] = cz[rows(z_all, 1), :] + hi
        d[rows(0, 1), :] = d[rows(0, 1), :] + lo
        d[rows(z_all - 1, 1), :] = d[rows(z_all - 1, 1), :] + hi

        def step(z, size):
            ch = jnp.where(outer, 0.5 * (get(name, z + 1, size) + edge_rows(name, z, size)), 0.0)
            diag = get("d" + k_, z, size) + ch
            put("ch" + k_, z, size, ch)
            put("d" + k_, z, size, diag)
            put("w" + k_, z, size, RELAX_WEIGHT / diag)

        chunks(z_all, step)

    def inner_terms(k, name):
        s = 1 << k
        k_ = str(k)

        def step(z, size):
            v = get(name, z + 1, size)
            t = get("g" + k_, z, size)
            t = t + get("cz" + k_, z, size) * get(name, z, size)
            t = t + get("cz" + k_, z + 1, size) * get(name, z + 2, size)
            t = t + get("cym" + k_, z, size) * pltpu.roll(v, s, 2)
            t = t + get("cyp" + k_, z, size) * pltpu.roll(v, lanes - s, 2)
            t = t + get("cxm" + k_, z, size) * pltpu.roll(v, s, 1)
            t = t + get("cxp" + k_, z, size) * pltpu.roll(v, SUB - s, 1)
            put("t" + k_, z, size, t)

        chunks(depth >> k, step)

    def with_halo(k, name, use, coarse=None):
        z_all = depth >> k
        k_ = str(k)
        t, cz, hz = m["t" + k_], m["cz" + k_], m["hz_" + name]
        arrive(name)
        if coarse is None:
            lo, hi = hz[0], hz[1]
        else:
            arrive(coarse)
            lo, hi = hz[0] + m["hz_" + coarse][0], hz[1] + m["hz_" + coarse][1]
        t[rows(0, 1), :] = t[rows(0, 1), :] + cz[rows(0, 1), :] * lo
        t[rows(z_all - 1, 1), :] = t[rows(z_all - 1, 1), :] + cz[rows(z_all, 1), :] * hi

        def step(z, size):
            use(z, size, get("t" + k_, z, size) + get("ch" + k_, z, size) * edge_rows(name, z, size, coarse))

        chunks(z_all, step)

    def relaxed(k, name, store, halo=None, coarse=None):
        k_ = str(k)

        def use(z, size, total):
            store(z, size, KEEP * get(name, z + 1, size) + get("w" + k_, z, size) * total)

        with_halo(k, halo or name, use, coarse)

    loads[0].wait()
    loads[1].wait()
    greeted = jnp.minimum(p, far) + jnp.minimum(planes - 1 - p, far) + peers - 1
    pl.semaphore_wait(barrier, greeted)
    exchange("b0", m["b0"])
    exchange("vin", m["vin"])
    for k in range(2):
        def coarser(z, size, k=k):
            half = z // 2
            put("b" + str(k + 1), half + 1, size // 2, 0.125 * restrict(get("b" + str(k), z + 1, size), k))
        chunks(depth >> k, coarser)
        exchange("b" + str(k + 1), m["b" + str(k + 1)])
    gather("gb", 0.125 * restrict(get("b2", 1, depth >> 2), 2))

    inner_coefficients(0)
    loads[2].wait()
    inner_terms(0, "vin")
    finish_coefficients(0)
    relaxed(0, "vin", lambda z, size, value: put("v0", z + 1, size, value))
    exchange("v0", m["v0"])
    inner_terms(0, "v0")
    inner_coefficients(1)
    finish_coefficients(1)
    bc = column("gb")
    side("bc", bc)

    def down(k, name):
        k_, n_ = str(k), str(k + 1)

        def use(z, size, total):
            r = total - get("d" + k_, z, size) * get(name, z + 1, size)
            g = 0.5 * restrict(r, k)
            if k == 2:
                gather("gf", g)
                return
            half = z // 2
            put("g" + n_, half, size // 2, g)
            put("v" + n_, half + 1, size // 2, g * get("w" + n_, half, size // 2))

        with_halo(k, name, use)

    down(0, "v0")
    exchange("v1", m["v1"])
    inner_terms(1, "v1")
    inner_coefficients(2)
    finish_coefficients(2)
    down(1, "v1")
    exchange("v2", m["v2"])
    inner_terms(2, "v2")

    reach = COARSE_SWEEPS + 1
    tall = 2 * peers
    lane_c = lax.broadcasted_iota(jnp.int32, (tall, NARROW), 1)
    row_c = lax.broadcasted_iota(jnp.int32, (tall, NARROW), 0)
    y_lo = jnp.logical_or(lane_c == 0, lane_c == 4)
    y_hi = jnp.logical_or(lane_c == NARROW - 5, lane_c == NARROW - 1)
    z_lo, z_hi = row_c == 0, row_c == tall - 1

    def before_y(v):
        return jnp.where(lane_c < 8, pltpu.roll(v, 9, 1), pltpu.roll(v, 8, 1))

    def after_y(v):
        return jnp.where(lane_c >= NARROW - 8, pltpu.roll(v, NARROW - 9, 1), pltpu.roll(v, NARROW - 8, 1))

    arrive("bc")
    b = {o: 0.5 * (bc if o == 0 else side_column("bc", o)) for o in range(-far, far + 1)}
    xp = {o: b[o] + b[o + 1] for o in range(-far, far)}
    ym, yp, zm, zp, diag, weight, inside = {}, {}, {}, {}, {}, {}, {}
    for o in range(-reach, reach + 1):
        ym[o] = b[o] + jnp.where(y_lo, 0.0, before_y(b[o]))
        yp[o] = b[o] + jnp.where(y_hi, 0.0, after_y(b[o]))
        zm[o] = b[o] + jnp.where(z_lo, 0.0, pltpu.roll(b[o], 1, 0))
        zp[o] = b[o] + jnp.where(z_hi, 0.0, pltpu.roll(b[o], tall - 1, 0))
        diag[o] = xp[o - 1] + xp[o] + ym[o] + yp[o] + zm[o] + zp[o]
        inside[o] = jnp.where(jnp.logical_and(p + o >= 0, p + o < planes), 1.0, 0.0).astype(jnp.float32)
        weight[o] = (RELAX_WEIGHT * inside[o]) / (diag[o] + (1.0 - inside[o]))
        ym[o], yp[o] = jnp.where(y_lo, 0.0, ym[o]), jnp.where(y_hi, 0.0, yp[o])
        zm[o], zp[o] = jnp.where(z_lo, 0.0, zm[o]), jnp.where(z_hi, 0.0, zp[o])
    share = {o: RELAX_WEIGHT * inside[o] / (jnp.sum(diag[o], axis=0, keepdims=True) + (1.0 - inside[o]))
             for o in (-1, 0, 1)}
    for o in range(3):
        m["col"][o, pl.ds(0, SUB), :] = jnp.zeros((SUB, NARROW), jnp.float32)
        m["col"][o, pl.ds(SUB + tall, SUB), :] = jnp.zeros((SUB, NARROW), jnp.float32)

    down(2, "v2")
    own_forcing = column("gf")
    side("fc", own_forcing)
    arrive("fc")
    forcing = {o: own_forcing if o == 0 else side_column("fc", o) for o in range(-reach, reach + 1)}
    guess = {o: weight[o] * forcing[o] for o in forcing}

    def total_of(o):
        v = guess[o]
        return (forcing[o] + xp[o - 1] * guess[o - 1] + xp[o] * guess[o + 1]
                + ym[o] * before_y(v) + yp[o] * after_y(v)
                + zm[o] * pltpu.roll(v, 1, 0) + zp[o] * pltpu.roll(v, tall - 1, 0))

    for wide in range(COARSE_SWEEPS, 1, -1):
        guess = {o: KEEP * guess[o] + weight[o] * total_of(o) for o in range(-wide, wide + 1)}
    for o in (-1, 0, 1):
        res_total = jnp.sum(total_of(o) - diag[o] * guess[o], axis=0, keepdims=True)
        m["col"][o + 1, pl.ds(SUB, tall), :] = guess[o] + share[o] * res_total

    for i, (o, j) in enumerate(((0, -1), (0, 0), (0, 1), (0, 2), (-1, 0), (-1, 1), (1, 0), (1, 1))):
        m["pick"][pl.ds(i, 1), :] = m["col"][o + 1, pl.ds(SUB + 2 * q + j, 1), :]
    m["wide"][...] = widen(m["pick"][...])

    def under(i):
        return m["wide"][pl.ds(i, 1), :]

    spread = lambda row: jnp.broadcast_to(row, (SUB, lanes))
    for j in range(depth >> 2):
        m["u2"][rows(j + 1, 1), :] = m["v2"][rows(j + 1, 1), :] + spread(under(1 + j // 2))
        m["hx_u2"][0, pl.ds(j, 1), :] = m["hx_v2"][0, pl.ds(j, 1), :] + under(4 + j // 2)
        m["hx_u2"][1, pl.ds(j, 1), :] = m["hx_v2"][1, pl.ds(j, 1), :] + under(6 + j // 2)
    m["hz_u2"][0] = m["hz_v2"][0] + spread(under(0))
    m["hz_u2"][1] = m["hz_v2"][1] + spread(under(3))
    inner_terms(2, "u2")
    relaxed(2, "u2", lambda z, size, value: put("r2", z + 1, size, value))
    exchange("r2", m["r2"])

    def add_coarse(k):
        fine, coarse, result = "v" + str(k), "r" + str(k + 1), "u" + str(k)

        def step(z, size):
            half = z // 2
            c = get(coarse, half + 1, size // 2)
            c = jnp.stack([c[i // 2] for i in range(size)])
            put(result, z + 1, size, get(fine, z + 1, size) + c)

        chunks(depth >> k, step)

    add_coarse(1)
    inner_terms(1, "u1")
    relaxed(1, "u1", lambda z, size, value: put("r1", z + 1, size, value), "v1", "r2")
    exchange("r1", m["r1"])

    add_coarse(0)
    inner_terms(0, "u0")

    def store(z, size, value):
        out[rows(z, size), :] = value.reshape(size * SUB, lanes)

    relaxed(0, "u0", store, "v0", "r1")
    for copy, sends in started:
        only(sends, lambda copy=copy: copy.wait_send())


def local(planes, peers, source, density, pressure):
    depth, width, lanes = source.shape
    flat = lambda x: x.reshape(depth * width, lanes)
    plan = scratch_plan(depth, lanes, peers)
    call = pl.pallas_call(
        functools.partial(cycle_kernel, tuple(plan), depth, lanes, planes, peers),
        out_shape=jax.ShapeDtypeStruct((depth * width, lanes), jnp.float32),
        in_specs=[pl.BlockSpec(memory_space=pl.ANY)] * 3,
        out_specs=pl.BlockSpec(memory_space=pltpu.VMEM),
        scratch_shapes=list(plan.values()),
        compiler_params=pltpu.CompilerParams(collective_id=0, has_side_effects=True, vmem_limit_bytes=GRANT),
        name="v_cycle",
    )
    return call(flat(source), flat(density), flat(pressure)).reshape(depth, width, lanes)


def solution(mesh):
    spec = P("vert", "plane", None)
    body = functools.partial(local, mesh.shape["plane"], mesh.shape["vert"])
    return jax.shard_map(body, mesh=mesh, in_specs=(spec, spec, spec), out_specs=spec, check_vma=False)
```

```python
import functools

import jax
import jax.numpy as jnp
from jax import lax
from jax.experimental import pallas as pl
from jax.experimental.pallas import tpu as pltpu
from jax.sharding import PartitionSpec as P

COARSE_SWEEPS = 4
RELAX_WEIGHT = 0.8
KEEP = 1.0 - RELAX_WEIGHT
MESH = pl.DeviceIdType.MESH
CHUNK = 16
SUB = 8
NARROW = 128
GRANT = 56170000

EXCHANGES = ("vin", "b0", "b1", "b2", "v0", "v1", "v2", "u2", "r2", "r1")
LEVEL_OF = {"vin": 0, "b0": 0, "b1": 1, "b2": 2, "v0": 0, "v1": 1, "v2": 2, "u2": 2, "u1": 1, "u0": 0, "r2": 2, "r1": 1}
SIDES = {"bc": COARSE_SWEEPS + 2, "fc": COARSE_SWEEPS + 1}
GATHERS = ("gb", "gf")


def scratch_plan(depth, lanes, peers):
    plan = {}
    field = lambda planes: pltpu.VMEM((planes * SUB, lanes), jnp.float32)
    for k in range(3):
        z = depth >> k
        for name in ("g", "t", "w", "d", "cym", "cyp", "cxm", "cxp", "ch"):
            plan[name + str(k)] = field(z)
        plan["cz" + str(k)] = field(z + 1)
        for name in ("b", "v", "u"):
            plan[name + str(k)] = field(z + 2)
    plan["vin"] = field(depth + 2)
    for name in EXCHANGES:
        z = depth >> LEVEL_OF[name]
        plan["hx_" + name] = pltpu.VMEM((2, z, lanes), jnp.float32)
        plan["sx_" + name] = pltpu.VMEM((2, z, lanes), jnp.float32)
        plan["hz_" + name] = pltpu.VMEM((2, SUB, lanes), jnp.float32)
    column = 2 * peers
    for name, reach in SIDES.items():
        plan["hx_" + name] = pltpu.VMEM((2 * reach + 1, SUB, NARROW), jnp.float32)
        plan["sx_" + name] = pltpu.VMEM((SUB, NARROW), jnp.float32)
    for name in GATHERS:
        plan["all_" + name] = pltpu.VMEM((peers * SUB, NARROW), jnp.float32)
        plan["own_" + name] = pltpu.VMEM((SUB, NARROW), jnp.float32)
    plan["r2"] = field((depth >> 2) + 2)
    plan["r1"] = field((depth >> 1) + 2)
    plan["col"] = pltpu.VMEM((3, column + 2 * SUB, NARROW), jnp.float32)
    plan["pick"] = pltpu.VMEM((SUB, NARROW), jnp.float32)
    plan["wide"] = pltpu.VMEM((SUB, lanes), jnp.float32)
    count = 4 * len(EXCHANGES) + 2 * sum(SIDES.values()) + (peers - 1) * len(GATHERS)
    plan["send"] = pltpu.SemaphoreType.DMA((count,))
    plan["recv"] = pltpu.SemaphoreType.DMA((count,))
    plan["load"] = pltpu.SemaphoreType.DMA((3,))
    return plan


def cycle_kernel(names, depth, lanes, planes, peers, source, density, pressure, out, *scratch):
    m = dict(zip(names, scratch))
    p, q = lax.axis_index("plane"), lax.axis_index("vert")
    left, right = lax.rem(p + planes - 1, planes), lax.rem(p + 1, planes)
    below, above = lax.rem(q + peers - 1, peers), lax.rem(q + 1, peers)
    has_left, has_right, has_below, has_above = p > 0, p < planes - 1, q > 0, q < peers - 1
    far = SIDES["bc"]

    loads = []
    for i, (src, dst) in enumerate(((density, m["b0"].at[pl.ds(SUB, SUB * depth)]),
                                    (pressure, m["vin"].at[pl.ds(SUB, SUB * depth)]),
                                    (source, m["g0"]))):
        loads.append(pltpu.make_async_copy(src, dst, m["load"].at[i]))
        loads[-1].start()

    barrier = pltpu.get_barrier_semaphore()
    for step in range(1, far + 1):
        @pl.when(p >= step)
        def _(step=step):
            pl.semaphore_signal(barrier, inc=1, device_id={"plane": p - step}, device_id_type=MESH)

        @pl.when(p + step < planes)
        def _(step=step):
            pl.semaphore_signal(barrier, inc=1, device_id={"plane": p + step}, device_id_type=MESH)
    for step in range(1, peers):
        pl.semaphore_signal(barrier, inc=1, device_id={"vert": lax.rem(q + step, peers)}, device_id_type=MESH)

    zero = jnp.zeros((SUB, lanes), jnp.float32)
    for name in ("vin", "v0", "v1", "v2", "u0", "u1", "u2", "b0", "b1", "b2"):
        z = depth >> LEVEL_OF[name]
        m[name][pl.ds(0, SUB), :] = zero
        m[name][pl.ds(SUB * (z + 1), SUB), :] = zero

    for name in EXCHANGES:
        for absent, half, slot in ((p == 0, "hx_", 0), (p == planes - 1, "hx_", 1),
                                   (q == 0, "hz_", 0), (q == peers - 1, "hz_", 1)):
            @pl.when(absent)
            def _(ref=m[half + name], slot=slot):
                ref[slot] = jnp.zeros(ref.shape[1:], jnp.float32)
    for name, reach in SIDES.items():
        for step in range(1, reach + 1):
            for absent, slot in ((p < step, reach - step), (p + step >= planes, reach + step)):
                @pl.when(absent)
                def _(ref=m["hx_" + name], slot=slot):
                    ref[slot] = jnp.zeros(ref.shape[1:], jnp.float32)

    lane = lax.broadcasted_iota(jnp.int32, (SUB, lanes), 1)
    sub = lax.broadcasted_iota(jnp.int32, (SUB, lanes), 0)

    used = [0]
    pending = {}
    started = []

    def only(condition, action):
        if condition is None:
            action()
        else:
            pl.when(condition)(action)

    def remote(key, src, dst, device, sends=None, receives=None):
        at = used[0]
        used[0] += 1
        copy = pltpu.make_async_remote_copy(
            src_ref=src, dst_ref=dst, send_sem=m["send"].at[at], recv_sem=m["recv"].at[at],
            device_id=device, device_id_type=MESH)
        only(sends, lambda: copy.start())
        pending.setdefault(key, []).append((copy, receives))
        started.append((copy, sends))

    def arrive(key):
        for copy, receives in pending.pop(key, ()):
            only(receives, lambda copy=copy: copy.wait_recv())

    def exchange(name, field):
        z = depth >> LEVEL_OF[name]
        hx, sx, hz = m["hx_" + name], m["sx_" + name], m["hz_" + name]
        for j in range(z):
            sx[0, pl.ds(j, 1), :] = field[pl.ds(SUB * (j + 1), 1), :]
            sx[1, pl.ds(j, 1), :] = field[pl.ds(SUB * (j + 2) - 1, 1), :]
        remote(name, sx.at[0], hx.at[1], {"plane": left}, has_left, has_right)
        remote(name, sx.at[1], hx.at[0], {"plane": right}, has_right, has_left)
        remote(name, field.at[pl.ds(SUB, SUB)], hz.at[1], {"vert": below}, has_below, has_above)
        remote(name, field.at[pl.ds(SUB * z, SUB)], hz.at[0], {"vert": above}, has_above, has_below)

    def side(name, value):
        reach = SIDES[name]
        sx, hx = m["sx_" + name], m["hx_" + name]
        sx[...] = jnp.where(twin, value[SUB:], value[:SUB])
        for step in range(1, reach + 1):
            lower, upper = lax.rem(p + planes - step, planes), lax.rem(p + step, planes)
            down, up = p >= step, p + step < planes
            remote(name, sx, hx.at[reach + step], {"plane": lower}, down, up)
            remote(name, sx, hx.at[reach - step], {"plane": upper}, up, down)

    quarter = lax.broadcasted_iota(jnp.int32, (SUB, NARROW), 1) & 3

    twin = (lax.broadcasted_iota(jnp.int32, (SUB, NARROW), 1) & 4) != 0

    def side_column(name, offset):
        both = m["hx_" + name][SIDES[name] + offset]
        top = jnp.where(twin, pltpu.roll(both, 4, 1), both)
        return jnp.concatenate([top, jnp.where(twin, both, pltpu.roll(both, NARROW - 4, 1))], axis=0)

    def narrow(tile):
        parts = [tile[:, NARROW * j:NARROW * (j + 1)] for j in range(lanes // NARROW)]
        return jnp.where(quarter == 0, parts[0], jnp.where(quarter == 1, parts[1],
                         jnp.where(quarter == 2, parts[2], parts[3])))

    def widen(tile):
        moved = {d: pltpu.roll(tile, (NARROW - d) % NARROW, 1) if d else tile for d in range(-3, 4)}
        return jnp.concatenate(
            [jnp.where(quarter == 0, moved[j], jnp.where(quarter == 1, moved[j - 1],
                       jnp.where(quarter == 2, moved[j - 2], moved[j - 3]))) for j in range(4)], axis=1)

    def gather(name, two):
        at = 2 * lax.rem(q, peers // 2)
        tile = narrow(jnp.where(sub == at, two[0], jnp.where(sub == at + 1, two[1], 0.0)))
        slot = pl.ds(pl.multiple_of(q * SUB, SUB), SUB)
        m["own_" + name][...] = tile
        for step in range(1, peers):
            remote(name, m["own_" + name], m["all_" + name].at[slot], {"vert": lax.rem(q + step, peers)})
        m["all_" + name][slot, :] = tile

    def column(name):
        arrive(name)
        parts = [m["all_" + name][pl.ds(SUB * i, SUB), :] for i in range(peers)]
        half = peers // 2
        return jnp.concatenate([sum(parts[1:half], parts[0]), sum(parts[half + 1:], parts[half])], axis=0)

    def chunks(z, step):
        size = min(CHUNK, z)
        if z == size:
            step(0, size)
        else:
            def run(i, carry):
                step(i * size, size)
                return carry
            lax.fori_loop(0, z // size, run, 0, unroll=True)

    def rows(z, size):
        start = SUB * z
        if not isinstance(z, int):
            start = pl.multiple_of(start, SUB)
        return pl.ds(start, SUB * size)

    def get(name, z, size):
        return m[name][rows(z, size), :].reshape(size, SUB, lanes)

    def put(name, z, size, value):
        m[name][rows(z, size), :] = value.reshape(size * SUB, lanes)

    def restrict(value, k):
        s = 1 << k
        n = value.shape[0]
        value = value.reshape(n // 2, 2, SUB, lanes)
        value = value[:, 0] + value[:, 1]
        value = value + jnp.where((lane & s) != 0, pltpu.roll(value, s, 2), pltpu.roll(value, lanes - s, 2))
        other = pltpu.roll(value, s, 1)
        if 2 * s != SUB:
            other = jnp.where((sub & s) != 0, other, pltpu.roll(value, SUB - s, 1))
        return value + other

    def edge_rows(name, z, size, coarse=None):
        hx = m["hx_" + name]
        result = []
        for j in range(size):
            lo, hi = hx[0, pl.ds(z + j, 1), :], hx[1, pl.ds(z + j, 1), :]
            if coarse is not None:
                below_it = pl.ds(z // 2 + j // 2, 1)
                lo, hi = lo + m["hx_" + coarse][0, below_it, :], hi + m["hx_" + coarse][1, below_it, :]
            lo, hi = jnp.broadcast_to(lo, (SUB, lanes)), jnp.broadcast_to(hi, (SUB, lanes))
            result.append(jnp.where(sub < SUB // 2, lo, hi))
        return jnp.stack(result)

    def inner_coefficients(k):
        s = 1 << k
        z_all = depth >> k
        name, k_ = "b" + str(k), str(k)
        ends_y = jnp.logical_or(lane < s, lane >= lanes - s)

        def step(z, size):
            b = 0.5 * get(name, z + 1, size)
            zm = b + 0.5 * get(name, z, size)
            zp = b + 0.5 * get(name, z + 2, size)
            ym = jnp.where(lane < s, 0.0, b + pltpu.roll(b, s, 2))
            yp = jnp.where(lane >= lanes - s, 0.0, b + pltpu.roll(b, lanes - s, 2))
            xm = jnp.where(sub < s, 0.0, b + pltpu.roll(b, s, 1))
            xp = jnp.where(sub >= SUB - s, 0.0, b + pltpu.roll(b, SUB - s, 1))
            put("cz" + k_, z, size, zm)
            put("cym" + k_, z, size, ym)
            put("cyp" + k_, z, size, yp)
            put("cxm" + k_, z, size, xm)
            put("cxp" + k_, z, size, xp)
            put("d" + k_, z, size, zm + zp + ym + yp + xm + xp + jnp.where(ends_y, b, 0.0))

        chunks(z_all, step)
        m["cz" + k_][rows(z_all, 1), :] = 0.5 * m[name][rows(z_all, 1), :]

    def finish_coefficients(k):
        s = 1 << k
        z_all = depth >> k
        name, k_ = "b" + str(k), str(k)
        cz, d, hz = m["cz" + k_], m["d" + k_], m["hz_" + name]
        outer = jnp.logical_or(sub < s, sub >= SUB - s)
        arrive(name)
        lo, hi = 0.5 * hz[0], 0.5 * hz[1]
        cz[rows(0, 1), :] = cz[rows(0, 1), :] + lo
        cz[rows(z_all, 1), :] = cz[rows(z_all, 1), :] + hi
        d[rows(0, 1), :] = d[rows(0, 1), :] + lo
        d[rows(z_all - 1, 1), :] = d[rows(z_all - 1, 1), :] + hi

        def step(z, size):
            ch = jnp.where(outer, 0.5 * (get(name, z + 1, size) + edge_rows(name, z, size)), 0.0)
            diag = get("d" + k_, z, size) + ch
            put("ch" + k_, z, size, ch)
            put("d" + k_, z, size, diag)
            put("w" + k_, z, size, RELAX_WEIGHT / diag)

        chunks(z_all, step)

    def inner_terms(k, name):
        s = 1 << k
        k_ = str(k)

        def step(z, size):
            v = get(name, z + 1, size)
            t = get("g" + k_, z, size)
            t = t + get("cz" + k_, z, size) * get(name, z, size)
            t = t + get("cz" + k_, z + 1, size) * get(name, z + 2, size)
            t = t + get("cym" + k_, z, size) * pltpu.roll(v, s, 2)
            t = t + get("cyp" + k_, z, size) * pltpu.roll(v, lanes - s, 2)
            t = t + get("cxm" + k_, z, size) * pltpu.roll(v, s, 1)
            t = t + get("cxp" + k_, z, size) * pltpu.roll(v, SUB - s, 1)
            put("t" + k_, z, size, t)

        chunks(depth >> k, step)

    def with_halo(k, name, use, coarse=None):
        z_all = depth >> k
        k_ = str(k)
        t, cz, hz = m["t" + k_], m["cz" + k_], m["hz_" + name]
        arrive(name)
        if coarse is None:
            lo, hi = hz[0], hz[1]
        else:
            arrive(coarse)
            lo, hi = hz[0] + m["hz_" + coarse][0], hz[1] + m["hz_" + coarse][1]
        t[rows(0, 1), :] = t[rows(0, 1), :] + cz[rows(0, 1), :] * lo
        t[rows(z_all - 1, 1), :] = t[rows(z_all - 1, 1), :] + cz[rows(z_all, 1), :] * hi

        def step(z, size):
            use(z, size, get("t" + k_, z, size) + get("ch" + k_, z, size) * edge_rows(name, z, size, coarse))

        chunks(z_all, step)

    def relaxed(k, name, store, halo=None, coarse=None):
        k_ = str(k)

        def use(z, size, total):
            store(z, size, KEEP * get(name, z + 1, size) + get("w" + k_, z, size) * total)

        with_halo(k, halo or name, use, coarse)

    loads[0].wait()
    loads[1].wait()
    greeted = jnp.minimum(p, far) + jnp.minimum(planes - 1 - p, far) + peers - 1
    pl.semaphore_wait(barrier, greeted)
    exchange("b0", m["b0"])
    exchange("vin", m["vin"])
    for k in range(2):
        def coarser(z, size, k=k):
            half = z // 2
            put("b" + str(k + 1), half + 1, size // 2, 0.125 * restrict(get("b" + str(k), z + 1, size), k))
        chunks(depth >> k, coarser)
        exchange("b" + str(k + 1), m["b" + str(k + 1)])
    gather("gb", 0.125 * restrict(get("b2", 1, depth >> 2), 2))

    inner_coefficients(0)
    loads[2].wait()
    inner_terms(0, "vin")
    finish_coefficients(0)
    relaxed(0, "vin", lambda z, size, value: put("v0", z + 1, size, value))
    exchange("v0", m["v0"])
    inner_terms(0, "v0")
    inner_coefficients(1)
    finish_coefficients(1)
    bc = column("gb")
    side("bc", bc)

    def down(k, name):
        k_, n_ = str(k), str(k + 1)

        def use(z, size, total):
            r = total - get("d" + k_, z, size) * get(name, z + 1, size)
            g = 0.5 * restrict(r, k)
            if k == 2:
                gather("gf", g)
                return
            half = z // 2
            put("g" + n_, half, size // 2, g)
            put("v" + n_, half + 1, size // 2, g * get("w" + n_, half, size // 2))

        with_halo(k, name, use)

    down(0, "v0")
    exchange("v1", m["v1"])
    inner_terms(1, "v1")
    inner_coefficients(2)
    finish_coefficients(2)
    down(1, "v1")
    exchange("v2", m["v2"])
    inner_terms(2, "v2")

    reach = COARSE_SWEEPS + 1
    tall = 2 * peers
    lane_c = lax.broadcasted_iota(jnp.int32, (tall, NARROW), 1)
    row_c = lax.broadcasted_iota(jnp.int32, (tall, NARROW), 0)
    y_lo = jnp.logical_or(lane_c == 0, lane_c == 4)
    y_hi = jnp.logical_or(lane_c == NARROW - 5, lane_c == NARROW - 1)
    z_lo, z_hi = row_c == 0, row_c == tall - 1

    def before_y(v):
        return jnp.where(lane_c < 8, pltpu.roll(v, 9, 1), pltpu.roll(v, 8, 1))

    def after_y(v):
        return jnp.where(lane_c >= NARROW - 8, pltpu.roll(v, NARROW - 9, 1), pltpu.roll(v, NARROW - 8, 1))

    arrive("bc")
    b = {o: 0.5 * (bc if o == 0 else side_column("bc", o)) for o in range(-far, far + 1)}
    xp = {o: b[o] + b[o + 1] for o in range(-far, far)}
    ym, yp, zm, zp, diag, weight, inside = {}, {}, {}, {}, {}, {}, {}
    for o in range(-reach, reach + 1):
        ym[o] = b[o] + jnp.where(y_lo, 0.0, before_y(b[o]))
        yp[o] = b[o] + jnp.where(y_hi, 0.0, after_y(b[o]))
        zm[o] = b[o] + jnp.where(z_lo, 0.0, pltpu.roll(b[o], 1, 0))
        zp[o] = b[o] + jnp.where(z_hi, 0.0, pltpu.roll(b[o], tall - 1, 0))
        diag[o] = xp[o - 1] + xp[o] + ym[o] + yp[o] + zm[o] + zp[o]
        inside[o] = jnp.where(jnp.logical_and(p + o >= 0, p + o < planes), 1.0, 0.0).astype(jnp.float32)
        weight[o] = (RELAX_WEIGHT * inside[o]) / (diag[o] + (1.0 - inside[o]))
        ym[o], yp[o] = jnp.where(y_lo, 0.0, ym[o]), jnp.where(y_hi, 0.0, yp[o])
        zm[o], zp[o] = jnp.where(z_lo, 0.0, zm[o]), jnp.where(z_hi, 0.0, zp[o])
    share = {o: RELAX_WEIGHT * inside[o] / (jnp.sum(diag[o], axis=0, keepdims=True) + (1.0 - inside[o]))
             for o in (-1, 0, 1)}
    for o in range(3):
        m["col"][o, pl.ds(0, SUB), :] = jnp.zeros((SUB, NARROW), jnp.float32)
        m["col"][o, pl.ds(SUB + tall, SUB), :] = jnp.zeros((SUB, NARROW), jnp.float32)

    down(2, "v2")
    own_forcing = column("gf")
    side("fc", own_forcing)
    arrive("fc")
    forcing = {o: own_forcing if o == 0 else side_column("fc", o) for o in range(-reach, reach + 1)}
    guess = {o: weight[o] * forcing[o] for o in forcing}

    def total_of(o):
        v = guess[o]
        return (forcing[o] + xp[o - 1] * guess[o - 1] + xp[o] * guess[o + 1]
                + ym[o] * before_y(v) + yp[o] * after_y(v)
                + zm[o] * pltpu.roll(v, 1, 0) + zp[o] * pltpu.roll(v, tall - 1, 0))

    for wide in range(COARSE_SWEEPS, 1, -1):
        guess = {o: KEEP * guess[o] + weight[o] * total_of(o) for o in range(-wide, wide + 1)}
    for o in (-1, 0, 1):
        res_total = jnp.sum(total_of(o) - diag[o] * guess[o], axis=0, keepdims=True)
        m["col"][o + 1, pl.ds(SUB, tall), :] = guess[o] + share[o] * res_total

    for i, (o, j) in enumerate(((0, -1), (0, 0), (0, 1), (0, 2), (-1, 0), (-1, 1), (1, 0), (1, 1))):
        m["pick"][pl.ds(i, 1), :] = m["col"][o + 1, pl.ds(SUB + 2 * q + j, 1), :]
    m["wide"][...] = widen(m["pick"][...])

    def under(i):
        return m["wide"][pl.ds(i, 1), :]

    spread = lambda row: jnp.broadcast_to(row, (SUB, lanes))
    for j in range(depth >> 2):
        m["u2"][rows(j + 1, 1), :] = m["v2"][rows(j + 1, 1), :] + spread(under(1 + j // 2))
        m["hx_u2"][0, pl.ds(j, 1), :] = m["hx_v2"][0, pl.ds(j, 1), :] + under(4 + j // 2)
        m["hx_u2"][1, pl.ds(j, 1), :] = m["hx_v2"][1, pl.ds(j, 1), :] + under(6 + j // 2)
    m["hz_u2"][0] = m["hz_v2"][0] + spread(under(0))
    m["hz_u2"][1] = m["hz_v2"][1] + spread(under(3))
    inner_terms(2, "u2")
    relaxed(2, "u2", lambda z, size, value: put("r2", z + 1, size, value))
    exchange("r2", m["r2"])

    def add_coarse(k):
        fine, coarse, result = "v" + str(k), "r" + str(k + 1), "u" + str(k)

        def step(z, size):
            half = z // 2
            c = get(coarse, half + 1, size // 2)
            c = jnp.stack([c[i // 2] for i in range(size)])
            put(result, z + 1, size, get(fine, z + 1, size) + c)

        chunks(depth >> k, step)

    add_coarse(1)
    inner_terms(1, "u1")
    relaxed(1, "u1", lambda z, size, value: put("r1", z + 1, size, value), "v1", "r2")
    exchange("r1", m["r1"])

    add_coarse(0)
    inner_terms(0, "u0")

    def store(z, size, value):
        out[rows(z, size), :] = value.reshape(size * SUB, lanes)

    relaxed(0, "u0", store, "v0", "r1")
    for copy, sends in started:
        only(sends, lambda copy=copy: copy.wait_send())


def local(planes, peers, source, density, pressure):
    depth, width, lanes = source.shape
    flat = lambda x: x.reshape(depth * width, lanes)
    plan = scratch_plan(depth, lanes, peers)
    call = pl.pallas_call(
        functools.partial(cycle_kernel, tuple(plan), depth, lanes, planes, peers),
        out_shape=jax.ShapeDtypeStruct((depth * width, lanes), jnp.float32),
        in_specs=[pl.BlockSpec(memory_space=pl.ANY)] * 3,
        out_specs=pl.BlockSpec(memory_space=pltpu.VMEM),
        scratch_shapes=list(plan.values()),
        compiler_params=pltpu.CompilerParams(collective_id=0, has_side_effects=True, vmem_limit_bytes=GRANT),
        name="v_cycle",
    )
    return call(flat(source), flat(density), flat(pressure)).reshape(depth, width, lanes)


def solution(mesh):
    spec = P("vert", "plane", None)
    body = functools.partial(local, mesh.shape["plane"], mesh.shape["vert"])
    return jax.shard_map(body, mesh=mesh, in_specs=(spec, spec, spec), out_specs=spec, check_vma=False)
```
